256 devices in a mesh: stn: 2 (over core), tm: 32 (over x, z_hi, y), ct: 4 (over z_lo).
Axes of the slice: x: 4, y: 4, z: 8 (z_hi: 2, z_lo: 4; z = z_hi * 4 + z_lo), core: 2. Of those that a mesh axis runs over, the one named last changes fastest.
Arguments:
- voltages: bfloat16 [2, 64, 2097152], P(None, ('stn', 'ct'), 'tm'), may hold values from -128 to 127, as said below
- delays: int32 [64], P(('stn', 'ct')), may hold values from 0 to 4095
Outputs:
- visibilities: float32 [2, 4096, 64, 64], P(None, ('tm', 'ct'), 'stn')
The draws below stay inside these ranges and needn't reach their ends.
Inputs may be any that keep to these rules, and one draw needn't show every extreme that they name: `voltages`: every entry is a whole number.
All inputs are finite; a program needn't handle non-finite values.
Results may differ from the reference program's by a relative error of at most 0.0037.
Values may be sent and summed in bfloat16 or wider, within the bound.
A program may use at most 128 MiB of HBM per device.

```python
import math
import jax
import jax.numpy as jnp
from jax import lax

CHANNELS = 4096
RADIX = 64
TAPS = 16
INPUTS = 64
FRAMES = 512
SAMPLES = 2097152


def draw_voltages(key, part):
    values = jax.random.randint(key, (2, INPUTS, SAMPLES), -128, 128).astype(jnp.float32)
    return values.astype(jnp.bfloat16)


def draw_delays(key, part):
    values = jax.random.randint(key, (INPUTS,), 0, CHANNELS)
    where_top = jax.random.randint(jax.random.fold_in(key, 1), (), 0, INPUTS)
    step_off = jax.random.randint(jax.random.fold_in(key, 2), (), 1, INPUTS)
    where_low = (where_top + step_off) % INPUTS
    index = jnp.arange(INPUTS, dtype=jnp.int32)
    values = jnp.where(index == where_top, CHANNELS - 1, values)
    values = jnp.where(index == where_low, 0, values)
    return values.astype(jnp.int32)


def setup_inputs(seed: int = 0) -> dict:
    key_of = jax.random.split(jax.random.key(seed), 3)
    return {
        "voltages": draw_voltages(jax.random.fold_in(key_of[2], 71), 0),
        "delays": draw_delays(jax.random.fold_in(key_of[2], 71), 0),
    }


def filter_table():
    length = TAPS * CHANNELS
    index = jnp.arange(length, dtype=jnp.int32).astype(jnp.float32)
    centred = (index - length / 2) / CHANNELS
    window = 0.5 - 0.5 * jnp.cos(2.0 * math.pi * index / length)
    factor = 1.0 / (48.0 * math.sqrt(CHANNELS))
    return (jnp.sinc(centred) * window * factor).reshape(TAPS, CHANNELS)

def dft_block(radix):
    steps = jnp.arange(radix, dtype=jnp.int32)
    grid = steps[:, None] * steps[None, :] % radix
    angle = 2.0 * math.pi * grid.astype(jnp.float32) / radix
    cosine = jnp.cos(angle)
    sine = jnp.sin(angle)
    upper = jnp.concatenate([cosine, sine], axis=1)
    lower = jnp.concatenate([-sine, cosine], axis=1)
    return jnp.concatenate([upper, lower], axis=0).astype(jnp.bfloat16)

def twiddles():
    second = CHANNELS // RADIX
    rows = jnp.arange(second, dtype=jnp.int32)
    cols = jnp.arange(RADIX, dtype=jnp.int32)
    grid = rows[:, None] * cols[None, :] % CHANNELS
    angle = 2.0 * math.pi * grid.astype(jnp.float32) / CHANNELS
    return (jnp.cos(angle), jnp.sin(angle))

def filtered(framed, table):
    count = framed.shape[-2] - TAPS + 1
    total = jnp.zeros(framed.shape[:-2] + (count, CHANNELS), jnp.float32)
    for tap in range(TAPS):
        begin = TAPS - 1 - tap
        total = total + table[tap] * framed[..., begin:begin + count, :].astype(jnp.float32)
    return total.astype(jnp.bfloat16)

def transform(branches):
    second = CHANNELS // RADIX
    number = branches.shape[0]
    stacked = branches.reshape(number, 2 * second, RADIX).astype(jnp.float32)
    first_table = dft_block(second).astype(jnp.float32)
    inner = jnp.einsum('kj,nja->nka', first_table, stacked, precision=lax.Precision.HIGHEST)
    inner = inner.reshape(number, 2, second, RADIX)
    tw_cos, tw_sin = twiddles()
    real_part = inner[:, 0] * tw_cos + inner[:, 1] * tw_sin
    imag_part = inner[:, 1] * tw_cos - inner[:, 0] * tw_sin
    turned = jnp.stack([real_part, imag_part], axis=2).reshape(number, second, 2 * RADIX)
    turned = turned.astype(jnp.bfloat16).astype(jnp.float32)
    last_table = dft_block(RADIX).astype(jnp.float32)
    result = jnp.einsum('lj,nkj->nlk', last_table, turned, precision=lax.Precision.HIGHEST)
    return result.reshape(number, 2, CHANNELS).astype(jnp.bfloat16)

def one_input(pair):
    signal, offset = pair
    table = filter_table()
    padded = jnp.concatenate([jnp.zeros((2, TAPS * CHANNELS), jnp.bfloat16), signal], axis=1)
    span = (FRAMES + TAPS - 1) * CHANNELS
    shifted = lax.dynamic_slice_in_dim(padded, (CHANNELS - offset).astype(jnp.int32), span, 1)
    framed = shifted.reshape(2, FRAMES + TAPS - 1, CHANNELS)
    branches = jnp.moveaxis(filtered(framed, table), 0, 1)
    return transform(branches)

def reference(voltages, delays):
    spectra = lax.map(one_input, (jnp.moveaxis(voltages, 1, 0), delays))
    block = min(CHANNELS, 128)
    starts = jnp.arange(CHANNELS // block, dtype=jnp.int32) * block

    def block_vis(start):
        piece = lax.dynamic_slice_in_dim(spectra, start, block, 3).astype(jnp.float32)
        swapped = jnp.stack([piece[:, :, 1], -piece[:, :, 0]], axis=2)
        left = jnp.stack([piece, swapped], axis=0)
        summed = jnp.einsum('oafjc,bfjc->ocab', left, piece, precision=lax.Precision.HIGHEST)
        return summed * (1.0 / FRAMES)
    blocks = lax.map(block_vis, starts)
    return blocks.transpose(1, 0, 2, 3, 4).reshape(2, CHANNELS, INPUTS, INPUTS)
```

```python
import math

import jax
import jax.numpy as jnp
import numpy as np
from jax import lax
from jax.experimental import pallas as pl
from jax.experimental.pallas import tpu as pltpu
from jax.sharding import PartitionSpec as P

CHANNELS = 4096
TAPS = 16
SLOW = 32
FAST = 128
BLOCK = 16
GROUP = 4
FRAMES = 512


def filter_table():
    length = TAPS * CHANNELS
    index = np.arange(length, dtype=np.float64)
    centred = (index - length / 2) / CHANNELS
    window = 0.5 - 0.5 * np.cos(2.0 * math.pi * index / length)
    factor = 1.0 / (48.0 * math.sqrt(CHANNELS))
    return (np.sinc(centred) * window * factor).reshape(TAPS, CHANNELS).astype(np.float32)


def rolled_filter(delay):
    table = filter_table()
    doubled = jnp.asarray(np.concatenate([table, table], axis=1))
    turned = lax.dynamic_slice(doubled, (0, delay), (TAPS, CHANNELS))
    carry = jnp.arange(CHANNELS, dtype=jnp.int32) + delay >= CHANNELS
    later = jnp.pad(turned, ((1, 7), (0, 0)))
    same = jnp.pad(turned, ((0, 8), (0, 0)))
    taps = jnp.where(carry[None, :], later, same)
    return taps.reshape(24, SLOW, FAST).transpose(1, 0, 2)


def turn_tables(delay):
    k = jnp.arange(SLOW, dtype=jnp.int32)[:, None]
    q = jnp.arange(FAST, dtype=jnp.int32)[None, :]
    angle = (k * (q + delay) % CHANNELS).astype(jnp.float32) * (2.0 * math.pi / CHANNELS)
    return jnp.stack([jnp.cos(angle), jnp.sin(angle)])


def last_table(delay):
    l = jnp.arange(FAST, dtype=jnp.int32)[:, None]
    q = jnp.arange(FAST, dtype=jnp.int32)[None, :]
    angle = (l * (q + delay) % FAST).astype(jnp.float32) * (2.0 * math.pi / FAST)
    cosine, sine = jnp.cos(angle), jnp.sin(angle)
    upper = jnp.concatenate([cosine, sine], axis=1)
    lower = jnp.concatenate([-sine, cosine], axis=1)
    return jnp.concatenate([upper, lower], axis=0).astype(jnp.bfloat16)


def fft(xs):
    n = len(xs)
    if n == 1:
        return xs
    even, odd = fft(xs[0::2]), fft(xs[1::2])
    low, high = [], []
    for k in range(n // 2):
        re, im = odd[k]
        if k == 0:
            tr, ti = re, im
        elif 4 * k == n:
            tr, ti = im, -re
        elif 8 * k == n:
            s = math.sqrt(0.5)
            tr, ti = (re + im) * s, (im - re) * s
        elif 8 * k == 3 * n:
            s = math.sqrt(0.5)
            tr, ti = (im - re) * s, (im + re) * (-s)
        else:
            c, s = math.cos(2 * math.pi * k / n), math.sin(2 * math.pi * k / n)
            tr, ti = re * c + im * s, im * c - re * s
        er, ei = even[k]
        low.append((er + tr, ei + ti))
        high.append((er - tr, ei - ti))
    return low + high


def spectra_kernel(own_ref, halo_ref, taps_ref, turn_ref, last_ref, out_ref, xs, branch, inner, flat):
    @pl.loop(0, 2)
    def _(i):
        @pl.loop(0, SLOW)
        def _(b):
            lanes = pl.ds(pl.multiple_of(b * FAST, FAST), FAST)
            taps = [
                jnp.broadcast_to(taps_ref[i, b, k : k + 1, :], (8, FAST)) for k in range(TAPS + 1)
            ]
            for r in range(2):
                xs[r, 0:BLOCK, :] = halo_ref[i, r, :, lanes].astype(jnp.float32)
                for g in range(GROUP):
                    first = BLOCK * (g + 1)
                    xs[r, first : first + BLOCK, :] = own_ref[g, i, r, :, lanes].astype(jnp.float32)
            for r in range(2):
                total = [None] * 8
                for s in range(-16, 57):
                    window = xs[r, BLOCK + s : BLOCK + s + 8, :]
                    for o in range(8):
                        k = 8 * o - s
                        if 0 <= k <= TAPS:
                            term = taps[k] * window
                            total[o] = term if total[o] is None else total[o] + term
                        if k == 0:
                            branch[r, b, 8 * o : 8 * o + 8, :] = total[o]

        @pl.loop(0, 8)
        def _(o):
            rows = pl.ds(pl.multiple_of(o * 8, 8), 8)
            points = [(branch[0, b, rows, :], branch[1, b, rows, :]) for b in range(SLOW)]
            for k, (re, im) in enumerate(fft(points)):
                c = jnp.broadcast_to(turn_ref[i, 0, k : k + 1, :], (8, FAST))
                s = jnp.broadcast_to(turn_ref[i, 1, k : k + 1, :], (8, FAST))
                inner[k, rows, 0:FAST] = re * c + im * s
                inner[k, rows, FAST : 2 * FAST] = im * c - re * s

        @pl.loop(0, 8)
        def _(g):
            points = inner[pl.ds(g * 4, 4), :, :].reshape(4 * 64, 2 * FAST).astype(jnp.bfloat16)
            result = lax.dot_general(
                last_ref[i], points, (((1,), (1,)), ((), ())), preferred_element_type=jnp.float32
            )
            for r in range(2):
                for t in range(2):
                    for l in range(16):
                        piece = result[
                            r * FAST + 8 * l : r * FAST + 8 * l + 8, t * FAST : t * FAST + FAST
                        ]
                        flat[r, pl.ds(l * 128 + g * 2 + t, 8, stride=16), :] = piece

        @pl.loop(0, FAST, step=8)
        def _(l0):
            for dl in range(8):
                for r in range(2):
                    rows = pl.ds(pl.multiple_of((l0 + dl) * 16, 16), 16)
                    out_ref[l0 + dl, i, r, :, :] = flat[r, rows, :].astype(jnp.bfloat16)


def spectra_of(own, halo, taps, turn, last):
    return pl.pallas_call(
        spectra_kernel,
        out_shape=jax.ShapeDtypeStruct((FAST, 2, 2, 16, FAST), jnp.bfloat16),
        in_specs=[pl.BlockSpec(memory_space=pltpu.VMEM)] * 5,
        out_specs=pl.BlockSpec(memory_space=pltpu.VMEM),
        scratch_shapes=[
            pltpu.VMEM((2, 80, FAST), jnp.float32),
            pltpu.VMEM((2, SLOW, 64, FAST), jnp.float32),
            pltpu.VMEM((SLOW, 64, 2 * FAST), jnp.float32),
            pltpu.VMEM((2, FAST * 16, FAST), jnp.float32),
        ],
        compiler_params=pltpu.CompilerParams(vmem_limit_bytes=48 << 20),
    )(own, halo, taps, turn, last)


def correlate_kernel(got_ref, out_ref, wide, packed):
    mine = lax.axis_index("stn")
    low = lax.broadcasted_iota(jnp.int32, (16, FAST), 1) < 64

    @pl.loop(0, 4)
    def _(pair):
        @pl.loop(0, 2)
        def _(t):
            @pl.loop(0, 2)
            def _(stn):
                for ct in range(4):
                    for y in range(4):
                        for i in range(2):
                            for r in range(2):
                                row = stn * 32 + (ct * 4 + y) * 2 + i
                                source = (pair * 2 + t) * 16 + y * 4 + ct
                                place = pl.ds(pl.multiple_of(row * 16, 16), 16)
                                wide[t, r, place, :] = got_ref[stn, source, i, r, :, :].astype(
                                    jnp.float32
                                )

        @pl.loop(0, 16)
        def _(j):
            for r in range(2):
                for g in range(4):
                    a = jnp.concatenate(
                        [wide[0, r, pl.ds((g * 16 + h * 8) * 16 + j, 8, stride=16), :] for h in range(2)],
                        axis=0,
                    )
                    b = jnp.concatenate(
                        [wide[1, r, pl.ds((g * 16 + h * 8) * 16 + j, 8, stride=16), :] for h in range(2)],
                        axis=0,
                    )
                    lanes = pl.ds(pl.multiple_of(pair * FAST, FAST), FAST)
                    place = slice(r * 64 + g * 16, r * 64 + g * 16 + 16)
                    packed[2 * j, place, lanes] = jnp.where(low, a, pltpu.roll(b, 64, 1)).astype(
                        jnp.bfloat16
                    )
                    packed[2 * j + 1, place, lanes] = jnp.where(low, pltpu.roll(a, 64, 1), b).astype(
                        jnp.bfloat16
                    )

    @pl.loop(0, SLOW)
    def _(k):
        everyone = packed[k]
        left = jnp.concatenate(
            [packed[k, pl.ds(pl.multiple_of(r * 64 + mine * 32, 32), 32), :] for r in range(2)], axis=0
        )
        grid = lax.dot_general(
            left, everyone, (((1,), (1,)), ((), ())), preferred_element_type=jnp.float32
        )
        out_ref[0, k, :, :] = (grid[0:32, 0:64] + grid[32:64, 64:128]) * (1.0 / FRAMES)
        out_ref[1, k, :, :] = (grid[32:64, 0:64] - grid[0:32, 64:128]) * (1.0 / FRAMES)


def correlated(got):
    return pl.pallas_call(
        correlate_kernel,
        out_shape=jax.ShapeDtypeStruct((2, SLOW, 32, 64), jnp.float32),
        in_specs=[pl.BlockSpec(memory_space=pltpu.VMEM)],
        out_specs=pl.BlockSpec(memory_space=pltpu.VMEM),
        scratch_shapes=[
            pltpu.VMEM((2, 2, 64 * 16, FAST), jnp.float32),
            pltpu.VMEM((SLOW, FAST, 4 * FAST), jnp.bfloat16),
        ],
        compiler_params=pltpu.CompilerParams(vmem_limit_bytes=48 << 20),
    )(got)


def on_device(voltages, delays):
    where = lax.axis_index("tm") % GROUP
    mine = lax.dynamic_slice(delays, (2 * where,), (2,))
    taps = jnp.stack([rolled_filter(mine[i]) for i in range(2)])
    turn = jnp.stack([turn_tables(mine[i]) for i in range(2)])
    last = jnp.stack([last_table(mine[i]) for i in range(2)])
    pieces = voltages.reshape(2, GROUP, 2, BLOCK, CHANNELS).transpose(1, 2, 0, 3, 4)
    groups = [[GROUP * g + j for j in range(GROUP)] for g in range(8)]
    own = lax.all_to_all(pieces, "tm", 0, 0, axis_index_groups=groups, tiled=True)
    halo = lax.ppermute(own[GROUP - 1], "tm", [(t, t + GROUP) for t in range(28)])
    chunks = spectra_of(own, halo, taps, turn, last)
    moved = lax.all_to_all(chunks, ("tm", "ct"), 0, 0, tiled=True)
    return correlated(lax.all_gather(moved, "stn", axis=0))


def solution(mesh):
    return jax.shard_map(
        on_device,
        mesh=mesh,
        in_specs=(P(None, ("stn", "ct"), "tm"), P(("stn", "ct"))),
        out_specs=P(None, ("tm", "ct"), "stn", None),
        check_vma=False,
    )
```

```python
import math

import jax
import jax.numpy as jnp
import numpy as np
from jax import lax
from jax.experimental import pallas as pl
from jax.experimental.pallas import tpu as pltpu
from jax.sharding import PartitionSpec as P

CHANNELS = 4096
TAPS = 16
SLOW = 32
FAST = 128
BLOCK = 16
GROUP = 4
FRAMES = 512
OWNERS = 128
MESH = pl.DeviceIdType.MESH


def filter_table():
    length = TAPS * CHANNELS
    index = np.arange(length, dtype=np.float64)
    centred = (index - length / 2) / CHANNELS
    window = 0.5 - 0.5 * np.cos(2.0 * math.pi * index / length)
    factor = 1.0 / (48.0 * math.sqrt(CHANNELS))
    return (np.sinc(centred) * window * factor).reshape(TAPS, CHANNELS).astype(np.float32)


def rolled_filter(delay):
    table = filter_table()
    doubled = jnp.asarray(np.concatenate([table, table], axis=1))
    turned = lax.dynamic_slice(doubled, (0, delay), (TAPS, CHANNELS))
    carry = jnp.arange(CHANNELS, dtype=jnp.int32) + delay >= CHANNELS
    later = jnp.pad(turned, ((1, 7), (0, 0)))
    same = jnp.pad(turned, ((0, 8), (0, 0)))
    taps = jnp.where(carry[None, :], later, same)
    return taps.reshape(24, SLOW, FAST).transpose(1, 0, 2)


def turn_tables(delay):
    k = jnp.arange(SLOW, dtype=jnp.int32)[:, None]
    q = jnp.arange(FAST, dtype=jnp.int32)[None, :]
    angle = (k * (q + delay) % CHANNELS).astype(jnp.float32) * (2.0 * math.pi / CHANNELS)
    return jnp.stack([jnp.cos(angle), jnp.sin(angle)])


def last_table(delay):
    l = jnp.arange(FAST, dtype=jnp.int32)[:, None]
    q = jnp.arange(FAST, dtype=jnp.int32)[None, :]
    angle = (l * (q + delay) % FAST).astype(jnp.float32) * (2.0 * math.pi / FAST)
    cosine, sine = jnp.cos(angle), jnp.sin(angle)
    upper = jnp.concatenate([cosine, sine], axis=1)
    lower = jnp.concatenate([-sine, cosine], axis=1)
    return jnp.concatenate([upper, lower], axis=0).astype(jnp.bfloat16)


def fft(xs):
    n = len(xs)
    if n == 1:
        return xs
    even, odd = fft(xs[0::2]), fft(xs[1::2])
    low, high = [], []
    for k in range(n // 2):
        re, im = odd[k]
        if k == 0:
            tr, ti = re, im
        elif 4 * k == n:
            tr, ti = im, -re
        elif 8 * k == n:
            s = math.sqrt(0.5)
            tr, ti = (re + im) * s, (im - re) * s
        elif 8 * k == 3 * n:
            s = math.sqrt(0.5)
            tr, ti = (im - re) * s, (im + re) * (-s)
        else:
            c, s = math.cos(2 * math.pi * k / n), math.sin(2 * math.pi * k / n)
            tr, ti = re * c + im * s, im * c - re * s
        er, ei = even[k]
        low.append((er + tr, ei + ti))
        high.append((er - tr, ei - ti))
    return low + high


def filter_and_transform(i, own, halo, taps_ref, turn_ref, last_ref, xs, branch, inner, flat):
    @pl.loop(0, SLOW)
    def _(b):
        lanes = pl.ds(pl.multiple_of(b * FAST, FAST), FAST)
        taps = [jnp.broadcast_to(taps_ref[i, b, k : k + 1, :], (8, FAST)) for k in range(TAPS + 1)]
        for r in range(2):
            xs[r, 0:BLOCK, :] = halo[i, r, :, lanes].astype(jnp.float32)
            for g in range(GROUP):
                first = BLOCK * (g + 1)
                xs[r, first : first + BLOCK, :] = own[g, i, r, :, lanes].astype(jnp.float32)
        for r in range(2):
            total = [None] * 8
            for s in range(-16, 57):
                window = xs[r, BLOCK + s : BLOCK + s + 8, :]
                for o in range(8):
                    k = 8 * o - s
                    if 0 <= k <= TAPS:
                        term = taps[k] * window
                        total[o] = term if total[o] is None else total[o] + term
                    if k == 0:
                        branch[r, b, 8 * o : 8 * o + 8, :] = total[o]

    @pl.loop(0, 8)
    def _(o):
        rows = pl.ds(pl.multiple_of(o * 8, 8), 8)
        points = [(branch[0, b, rows, :], branch[1, b, rows, :]) for b in range(SLOW)]
        for k, (re, im) in enumerate(fft(points)):
            c = jnp.broadcast_to(turn_ref[i, 0, k : k + 1, :], (8, FAST))
            s = jnp.broadcast_to(turn_ref[i, 1, k : k + 1, :], (8, FAST))
            inner[k, rows, 0:FAST] = re * c + im * s
            inner[k, rows, FAST : 2 * FAST] = im * c - re * s

    @pl.loop(0, 8)
    def _(g):
        points = inner[pl.ds(g * 4, 4), :, :].reshape(4 * 64, 2 * FAST).astype(jnp.bfloat16)
        result = lax.dot_general(
            last_ref[i], points, (((1,), (1,)), ((), ())), preferred_element_type=jnp.float32
        )
        for r in range(2):
            for t in range(2):
                for l in range(16):
                    piece = result[r * FAST + 8 * l : r * FAST + 8 * l + 8, t * FAST : t * FAST + FAST]
                    flat[r, pl.ds(l * 128 + g * 2 + t, 8, stride=16), :] = piece


def gather_pair(pair, got, wide, packed):
    low = lax.broadcasted_iota(jnp.int32, (8, FAST), 1) < 64

    @pl.loop(0, 4)
    def _(step):
        t = step // 2
        stn = step % 2
        for ct in range(4):
            for y in range(4):
                for i in range(2):
                    for r in range(2):
                        row = stn * 32 + (ct * 4 + y) * 2 + i
                        source = (pair * 2 + t) * 16 + y * 4 + ct
                        place = pl.ds(pl.multiple_of(row * 16, 16), 16)
                        wide[t, r, place, :] = got[stn, source, i, r, :, :].astype(jnp.float32)

    lanes = pl.ds(pl.multiple_of(pair * FAST, FAST), FAST)

    def reorder(j):
        for r in range(2):
            for g in range(4):
                even, odd = [], []
                for h in range(2):
                    rows = pl.ds((g * 16 + h * 8) * 16 + j, 8, stride=16)
                    a, b = wide[0, r, rows, :], wide[1, r, rows, :]
                    crossed = pltpu.roll(jnp.where(low, b, a), 64, 1)
                    even.append(jnp.where(low, a, crossed))
                    odd.append(jnp.where(low, crossed, b))
                place = slice(r * 64 + g * 16, r * 64 + g * 16 + 16)
                packed[2 * j, place, lanes] = jnp.concatenate(even, axis=0).astype(jnp.bfloat16)
                packed[2 * j + 1, place, lanes] = jnp.concatenate(odd, axis=0).astype(jnp.bfloat16)

    @pl.loop(0, 16, step=4)
    def _(j0):
        for u in range(4):
            reorder(j0 + u)


def correlate(mine, packed, out_ref):
    @pl.loop(0, SLOW, step=4)
    def _(k0):
        for u in range(4):
            k = k0 + u
            left = jnp.concatenate(
                [packed[k, pl.ds(pl.multiple_of(r * 64 + mine * 32, 32), 32), :] for r in range(2)],
                axis=0,
            )
            grid = lax.dot_general(
                left, packed[k], (((1,), (1,)), ((), ())), preferred_element_type=jnp.float32
            )
            out_ref[0, k, :, :] = (grid[0:32, 0:64] + grid[32:64, 64:128]) * (1.0 / FRAMES)
            out_ref[1, k, :, :] = (grid[32:64, 0:64] - grid[0:32, 64:128]) * (1.0 / FRAMES)


def whole_kernel(
    pieces,
    taps_ref,
    turn_ref,
    last_ref,
    out_ref,
    own,
    halo,
    chunks,
    got,
    xs,
    branch,
    inner,
    flat,
    wide,
    packed,
    near_send,
    near_recv,
    halo_send,
    halo_recv,
    far_send,
    far_recv,
    twin_send,
    twin_recv,
):
    tm, ct, stn = lax.axis_index("tm"), lax.axis_index("ct"), lax.axis_index("stn")
    me = tm * 4 + ct
    y, block, column = tm % 4, tm // 4, tm // 8

    barrier = pltpu.get_barrier_semaphore()

    @pl.loop(1, OWNERS)
    def _(j):
        l = (me + j) % OWNERS
        pl.semaphore_signal(
            barrier, inc=1, device_id={"tm": l // 4, "ct": l % 4}, device_id_type=MESH
        )

    pl.semaphore_signal(barrier, inc=1, device_id={"stn": 1 - stn}, device_id_type=MESH)

    @pl.when(block == 0)
    def _():
        halo[...] = jnp.zeros_like(halo)

    pl.semaphore_wait(barrier, OWNERS)

    def near(i, offset):
        other = (y + offset) % GROUP
        return pltpu.make_async_remote_copy(
            src_ref=pieces.at[other, i],
            dst_ref=own.at[y, i],
            send_sem=near_send.at[i, offset],
            recv_sem=near_recv.at[i, y],
            device_id={"tm": block * 4 + other},
            device_id_type=MESH,
        )

    def near_arrival(i, source):
        return pltpu.make_async_copy(pieces.at[0, i], own.at[source, i], near_recv.at[i, source])

    def halo_copy(i):
        return pltpu.make_async_remote_copy(
            src_ref=own.at[GROUP - 1, i],
            dst_ref=halo.at[i],
            send_sem=halo_send.at[i],
            recv_sem=halo_recv.at[i],
            device_id={"tm": (tm + GROUP) % 32},
            device_id_type=MESH,
        )

    for i in range(2):
        pltpu.make_async_copy(pieces.at[y, i], own.at[y, i], near_recv.at[i, y]).start()
        for offset in (1, 3, 2):
            near(i, offset).start()
    for i in range(2):
        near_arrival(i, GROUP - 1).wait()

        @pl.when(block < 7)
        def _():
            halo_copy(i).start()

    def far(l, i):
        return pltpu.make_async_remote_copy(
            src_ref=chunks.at[l, i],
            dst_ref=got.at[stn, me, i],
            send_sem=far_send,
            recv_sem=far_recv.at[column],
            device_id={"tm": l // 4, "ct": l % 4},
            device_id_type=MESH,
        )

    @pl.loop(0, 2)
    def _(i):
        for source in range(GROUP - 1):
            near_arrival(i, source).wait()

        @pl.when(block > 0)
        def _():
            halo_copy(i).wait_recv()

        filter_and_transform(i, own, halo, taps_ref, turn_ref, last_ref, xs, branch, inner, flat)

        @pl.loop(0, OWNERS, step=4)
        def _(j0):
            for u in range(4):
                l = (me + j0 + u) % OWNERS
                rows = pl.ds(pl.multiple_of(l * 16, 16), 16)
                for r in range(2):
                    chunks[l, i, r, :, :] = flat[r, rows, :].astype(jnp.bfloat16)

            @pl.when(j0 == 0)
            def _():
                pltpu.make_async_copy(
                    chunks.at[me, i], got.at[stn, me, i], far_recv.at[column]
                ).start()

            @pl.when(j0 > 0)
            def _():
                far((me + j0) % OWNERS, i).start()

            for u in range(1, 4):
                far((me + j0 + u) % OWNERS, i).start()

    def twin(p):
        rows = got.at[stn, pl.ds(p * 32, 32)]
        return pltpu.make_async_remote_copy(
            src_ref=rows,
            dst_ref=rows,
            send_sem=twin_send.at[p],
            recv_sem=twin_recv.at[p],
            device_id={"stn": 1 - stn},
            device_id_type=MESH,
        )

    def hand_over(p):
        rows = got.at[stn, pl.ds(p * 32, 32)]
        pltpu.make_async_copy(rows, rows, far_recv.at[p]).wait()
        twin(p).start()

    hand_over((column + 3) % 4)

    @pl.loop(0, 4)
    def _(step):
        p = (column + 3 - step) % 4

        @pl.when(step < 3)
        def _():
            hand_over((column + 2 - step + 4) % 4)

        twin(p).wait_recv()
        gather_pair(p, got, wide, packed)

    correlate(stn, packed, out_ref)

    for i in range(2):
        for offset in (1, 3, 2):
            near(i, offset).wait_send()

        @pl.when(block < 7)
        def _():
            halo_copy(i).wait_send()

    for p in range(4):
        twin(p).wait_send()
    sent = chunks.at[pl.ds(0, OWNERS - 1)]
    pltpu.make_async_copy(sent, sent, far_send).wait()


def on_device(voltages, delays):
    where = lax.axis_index("tm") % GROUP
    mine = lax.dynamic_slice(delays, (2 * where,), (2,))
    taps = jnp.stack([rolled_filter(mine[i]) for i in range(2)])
    turn = jnp.stack([turn_tables(mine[i]) for i in range(2)])
    last = jnp.stack([last_table(mine[i]) for i in range(2)])
    pieces = voltages.reshape(2, GROUP, 2, BLOCK, CHANNELS).transpose(1, 2, 0, 3, 4)
    dma = pltpu.SemaphoreType.DMA
    f32, bf16 = jnp.float32, jnp.bfloat16
    return pl.pallas_call(
        whole_kernel,
        out_shape=jax.ShapeDtypeStruct((2, SLOW, 32, 64), f32),
        in_specs=[pl.BlockSpec(memory_space=pltpu.VMEM)] * 4,
        out_specs=pl.BlockSpec(memory_space=pltpu.VMEM),
        scratch_shapes=[
            pltpu.VMEM((GROUP, 2, 2, BLOCK, CHANNELS), bf16),
            pltpu.VMEM((2, 2, BLOCK, CHANNELS), bf16),
            pltpu.VMEM((OWNERS, 2, 2, 16, FAST), bf16),
            pltpu.VMEM((2, OWNERS, 2, 2, 16, FAST), bf16),
            pltpu.VMEM((2, 80, FAST), f32),
            pltpu.VMEM((2, SLOW, 64, FAST), f32),
            pltpu.VMEM((SLOW, 64, 2 * FAST), f32),
            pltpu.VMEM((2, FAST * 16, FAST), f32),
            pltpu.VMEM((2, 2, 64 * 16, FAST), f32),
            pltpu.VMEM((SLOW, FAST, 4 * FAST), bf16),
            dma((2, GROUP)),
            dma((2, GROUP)),
            dma((2,)),
            dma((2,)),
            dma,
            dma((4,)),
            dma((4,)),
            dma((4,)),
        ],
        compiler_params=pltpu.CompilerParams(
            collective_id=0, has_side_effects=True, vmem_limit_bytes=56 << 20
        ),
    )(pieces, taps, turn, last)


def solution(mesh):
    return jax.shard_map(
        on_device,
        mesh=mesh,
        in_specs=(P(None, ("stn", "ct"), "tm"), P(("stn", "ct"))),
        out_specs=P(None, ("tm", "ct"), "stn", None),
        check_vma=False,
    )
```

```python
import math

import jax
import jax.numpy as jnp
import numpy as np
from jax import lax
from jax.experimental import pallas as pl
from jax.experimental.pallas import tpu as pltpu
from jax.sharding import PartitionSpec as P

CHANNELS = 4096
TAPS = 16
SLOW = 32
FAST = 128
BLOCK = 16
GROUP = 4
FRAMES = 512
OWNERS = 128
MESH = pl.DeviceIdType.MESH


def filter_table():
    length = TAPS * CHANNELS
    index = np.arange(length, dtype=np.float64)
    centred = (index - length / 2) / CHANNELS
    window = 0.5 - 0.5 * np.cos(2.0 * math.pi * index / length)
    factor = 1.0 / (48.0 * math.sqrt(CHANNELS))
    return (np.sinc(centred) * window * factor).reshape(TAPS, CHANNELS).astype(np.float32)


def tap_blocks():
    return filter_table().reshape(TAPS, SLOW, FAST).transpose(1, 0, 2)


def turn_blocks():
    angle = np.arange(SLOW)[:, None] * np.arange(CHANNELS)[None, :] % CHANNELS
    angle = angle * (2.0 * math.pi / CHANNELS)
    both = np.concatenate([np.cos(angle), np.sin(angle)]).astype(np.float32)
    return both.reshape(2 * SLOW, SLOW, FAST).transpose(1, 0, 2)


def last_table():
    angle = np.arange(FAST)[:, None] * np.arange(FAST)[None, :] % FAST * (2.0 * math.pi / FAST)
    cosine, sine = np.cos(angle), np.sin(angle)
    upper = np.concatenate([cosine, sine], axis=1)
    lower = np.concatenate([-sine, cosine], axis=1)
    return np.concatenate([upper, lower], axis=0).astype(np.float32)


def fft(xs):
    n = len(xs)
    if n == 1:
        return xs
    even, odd = fft(xs[0::2]), fft(xs[1::2])
    low, high = [], []
    for k in range(n // 2):
        re, im = odd[k]
        if k == 0:
            tr, ti = re, im
        elif 4 * k == n:
            tr, ti = im, -re
        elif 8 * k == n:
            s = math.sqrt(0.5)
            tr, ti = (re + im) * s, (im - re) * s
        elif 8 * k == 3 * n:
            s = math.sqrt(0.5)
            tr, ti = (im - re) * s, (im + re) * (-s)
        else:
            c, s = math.cos(2 * math.pi * k / n), math.sin(2 * math.pi * k / n)
            tr, ti = re * c + im * s, im * c - re * s
        er, ei = even[k]
        low.append((er + tr, ei + ti))
        high.append((er - tr, ei - ti))
    return low + high


def split_inputs(voltages, spread, pieces):
    @pl.loop(0, SLOW)
    def _(b):
        lanes = pl.ds(pl.multiple_of(b * FAST, FAST), FAST)
        for r in range(2):
            for f in range(BLOCK):
                there = pl.ds(pl.multiple_of(f * CHANNELS + b * FAST, FAST), FAST)
                spread[r, pl.ds(f, 8, stride=BLOCK), :] = voltages[r, :, there].astype(jnp.float32)
        for r in range(2):
            for i in range(8):
                rows = spread[r, BLOCK * i : BLOCK * i + BLOCK, :]
                pieces[i // 2, i % 2, r, :, lanes] = rows.astype(jnp.bfloat16)


def delayed_tables(i, delay, tap_ref, turn_all, last_all, taps_ref, turn_ref, last_ref):
    high, low = delay >> 7, delay & 127
    lane = lax.broadcasted_iota(jnp.int32, (1, FAST), 1)
    same = lane < FAST - low
    shift = (FAST - low) & 127

    def ahead(table, b):
        first = pltpu.roll(table[(b + high) & 31], shift, 1)
        second = pltpu.roll(table[(b + high + 1) & 31], shift, 1)
        return jnp.where(same, first, second)

    @pl.loop(0, SLOW)
    def _(b):
        rolled = ahead(tap_ref, b)
        carry = lane + b * FAST + delay >= CHANNELS
        taps_ref[i, b, 0:TAPS, :] = jnp.where(carry, 0.0, rolled)
        taps_ref[i, b, TAPS : TAPS + 8, :] = jnp.zeros((8, FAST), jnp.float32)
        taps_ref[i, b, 1 : TAPS + 1, :] += jnp.where(carry, rolled, 0.0)

    turn_ref[i] = ahead(turn_all, 0)

    @pl.loop(0, 8)
    def _(g):
        rows = pl.ds(pl.multiple_of(g * 32, 32), 32)
        for part in range(2):
            lanes = slice(part * FAST, part * FAST + FAST)
            last_ref[i, rows, lanes] = pltpu.roll(last_all[rows, lanes], shift, 1).astype(jnp.bfloat16)


def filter_frames(i, own, halo, taps_ref, xs, branch, first):
    octets = range(2) if first else range(2, 8)
    base = BLOCK if first else 0

    @pl.loop(0, SLOW)
    def _(b):
        lanes = pl.ds(pl.multiple_of(b * FAST, FAST), FAST)
        taps = [jnp.broadcast_to(taps_ref[i, b, k : k + 1, :], (8, FAST)) for k in range(TAPS + 1)]
        for r in range(2):
            if first:
                xs[r, 0:BLOCK, :] = halo[i, r, :, lanes].astype(jnp.float32)
                xs[r, BLOCK : 2 * BLOCK, :] = own[0, i, r, :, lanes].astype(jnp.float32)
            else:
                for g in range(GROUP):
                    xs[r, BLOCK * g : BLOCK * g + BLOCK, :] = own[g, i, r, :, lanes].astype(
                        jnp.float32
                    )
        for r in range(2):
            total = {}
            for s in range(8 * octets[0] - TAPS, 8 * octets[-1] + 1):
                window = xs[r, base + s : base + s + 8, :]
                for o in octets:
                    k = 8 * o - s
                    if 0 <= k <= TAPS:
                        term = taps[k] * window
                        total[o] = total[o] + term if o in total else term
                    if k == 0:
                        branch[r, b, 8 * o : 8 * o + 8, :] = total[o]


def slow_transform(i, turn_ref, branch, inner, first):
    @pl.loop(*((0, 2) if first else (2, 8)))
    def _(o):
        rows = pl.ds(pl.multiple_of(o * 8, 8), 8)
        points = [(branch[0, b, rows, :], branch[1, b, rows, :]) for b in range(SLOW)]
        for k, (re, im) in enumerate(fft(points)):
            c = jnp.broadcast_to(turn_ref[i, k : k + 1, :], (8, FAST))
            s = jnp.broadcast_to(turn_ref[i, SLOW + k : SLOW + k + 1, :], (8, FAST))
            inner[k, rows, 0:FAST] = re * c + im * s
            inner[k, rows, FAST : 2 * FAST] = im * c - re * s


def fast_transform(i, last_ref, inner, flat):
    @pl.loop(0, 8)
    def _(g):
        points = inner[pl.ds(g * 4, 4), :, :].reshape(4 * 64, 2 * FAST).astype(jnp.bfloat16)
        result = lax.dot_general(
            last_ref[i], points, (((1,), (1,)), ((), ())), preferred_element_type=jnp.float32
        )
        for r in range(2):
            for t in range(2):
                for l in range(16):
                    piece = result[r * FAST + 8 * l : r * FAST + 8 * l + 8, t * FAST : t * FAST + FAST]
                    flat[r, pl.ds(l * 128 + g * 2 + t, 8, stride=16), :] = piece


def gather_pair(pair, got, wide, packed):
    low = lax.broadcasted_iota(jnp.int32, (8, FAST), 1) < 64

    @pl.loop(0, 4)
    def _(step):
        t = step // 2
        stn = step % 2
        for ct in range(4):
            for y in range(4):
                for i in range(2):
                    for r in range(2):
                        row = stn * 32 + (ct * 4 + y) * 2 + i
                        source = (pair * 2 + t) * 16 + y * 4 + ct
                        place = pl.ds(pl.multiple_of(row * 16, 16), 16)
                        wide[t, r, place, :] = got[stn, source, i, r, :, :].astype(jnp.float32)

    lanes = pl.ds(pl.multiple_of(pair * FAST, FAST), FAST)

    def reorder(j):
        for r in range(2):
            for g in range(4):
                even, odd = [], []
                for h in range(2):
                    rows = pl.ds((g * 16 + h * 8) * 16 + j, 8, stride=16)
                    a, b = wide[0, r, rows, :], wide[1, r, rows, :]
                    crossed = pltpu.roll(jnp.where(low, b, a), 64, 1)
                    even.append(jnp.where(low, a, crossed))
                    odd.append(jnp.where(low, crossed, b))
                place = slice(r * 64 + g * 16, r * 64 + g * 16 + 16)
                packed[2 * j, place, lanes] = jnp.concatenate(even, axis=0).astype(jnp.bfloat16)
                packed[2 * j + 1, place, lanes] = jnp.concatenate(odd, axis=0).astype(jnp.bfloat16)

    @pl.loop(0, 16, step=4)
    def _(j0):
        for u in range(4):
            reorder(j0 + u)


def correlate(mine, packed, out_ref):
    @pl.loop(0, SLOW, step=4)
    def _(k0):
        for u in range(4):
            k = k0 + u
            left = jnp.concatenate(
                [packed[k, pl.ds(pl.multiple_of(r * 64 + mine * 32, 32), 32), :] for r in range(2)],
                axis=0,
            )
            grid = lax.dot_general(
                left, packed[k], (((1,), (1,)), ((), ())), preferred_element_type=jnp.float32
            )
            out_ref[0, k, :, :] = (grid[0:32, 0:64] + grid[32:64, 64:128]) * (1.0 / FRAMES)
            out_ref[1, k, :, :] = (grid[32:64, 0:64] - grid[0:32, 64:128]) * (1.0 / FRAMES)


def whole_kernel(
    delays,
    voltages_hbm,
    tap_hbm,
    turn_hbm,
    last_hbm,
    out_ref,
    voltages,
    tap_all,
    turn_all,
    last_all,
    taps_ref,
    turn_ref,
    last_ref,
    spread,
    pieces,
    own,
    halo,
    chunks,
    got,
    xs,
    branch,
    inner,
    flat,
    wide,
    packed,
    load_sem,
    near_send,
    near_recv,
    halo_send,
    halo_recv,
    far_send,
    far_recv,
    twin_send,
    twin_recv,
):
    tm, ct, stn = lax.axis_index("tm"), lax.axis_index("ct"), lax.axis_index("stn")
    me = tm * 4 + ct
    y, block, column = tm % 4, tm // 4, tm // 8

    loads = [
        pltpu.make_async_copy(voltages_hbm, voltages, load_sem.at[0]),
        pltpu.make_async_copy(tap_hbm, tap_all, load_sem.at[1]),
        pltpu.make_async_copy(turn_hbm, turn_all, load_sem.at[2]),
        pltpu.make_async_copy(last_hbm, last_all, load_sem.at[3]),
    ]
    for load in loads:
        load.start()

    barrier = pltpu.get_barrier_semaphore()

    @pl.loop(1, OWNERS)
    def _(j):
        l = (me + j) % OWNERS
        pl.semaphore_signal(
            barrier, inc=1, device_id={"tm": l // 4, "ct": l % 4}, device_id_type=MESH
        )

    pl.semaphore_signal(barrier, inc=1, device_id={"stn": 1 - stn}, device_id_type=MESH)

    @pl.when(block == 0)
    def _():
        halo[...] = jnp.zeros_like(halo)

    loads[0].wait()
    split_inputs(voltages, spread, pieces)
    pl.semaphore_wait(barrier, OWNERS)

    def near(i, r, offset):
        other = (y + offset) % GROUP
        return pltpu.make_async_remote_copy(
            src_ref=pieces.at[other, i, r],
            dst_ref=own.at[y, i, r],
            send_sem=near_send.at[i, r, offset],
            recv_sem=near_recv.at[i, r, y],
            device_id={"tm": block * 4 + other},
            device_id_type=MESH,
        )

    def near_arrival(i, r, source):
        return pltpu.make_async_copy(
            pieces.at[0, i, r], own.at[source, i, r], near_recv.at[i, r, source]
        )

    def halo_copy(i, r):
        return pltpu.make_async_remote_copy(
            src_ref=own.at[GROUP - 1, i, r],
            dst_ref=halo.at[i, r],
            send_sem=halo_send.at[i, r],
            recv_sem=halo_recv.at[i, r],
            device_id={"tm": (tm + GROUP) % 32},
            device_id_type=MESH,
        )

    def pass_on(i):
        for r in range(2):
            near_arrival(i, r, GROUP - 1).wait()

            @pl.when(block < 7)
            def _():
                halo_copy(i, r).start()

    for i in range(2):
        for r in range(2):
            pltpu.make_async_copy(
                pieces.at[y, i, r], own.at[y, i, r], near_recv.at[i, r, y]
            ).start()
            for offset in (1, 3, 2):
                near(i, r, offset).start()

    for load in loads[1:]:
        load.wait()
    for i in range(2):
        delayed_tables(
            i, delays[2 * y + i], tap_all, turn_all, last_all, taps_ref, turn_ref, last_ref
        )
        if i == 0:
            pass_on(0)

    def far(l, i):
        return pltpu.make_async_remote_copy(
            src_ref=chunks.at[l, i],
            dst_ref=got.at[stn, me, i],
            send_sem=far_send,
            recv_sem=far_recv.at[column],
            device_id={"tm": l // 4, "ct": l % 4},
            device_id_type=MESH,
        )

    @pl.loop(0, 2)
    def _(i):
        for r in range(2):
            for source in range(GROUP - 1):
                near_arrival(i, r, source).wait()

        filter_frames(i, own, halo, taps_ref, xs, branch, False)
        slow_transform(i, turn_ref, branch, inner, False)

        @pl.when(i == 0)
        def _():
            pass_on(1)

        @pl.when(block > 0)
        def _():
            for r in range(2):
                halo_copy(i, r).wait_recv()

        filter_frames(i, own, halo, taps_ref, xs, branch, True)
        slow_transform(i, turn_ref, branch, inner, True)
        fast_transform(i, last_ref, inner, flat)

        @pl.loop(0, OWNERS, step=4)
        def _(j0):
            for u in range(4):
                l = (me + j0 + u) % OWNERS
                rows = pl.ds(pl.multiple_of(l * 16, 16), 16)
                for r in range(2):
                    chunks[l, i, r, :, :] = flat[r, rows, :].astype(jnp.bfloat16)

            @pl.when(j0 == 0)
            def _():
                pltpu.make_async_copy(
                    chunks.at[me, i], got.at[stn, me, i], far_recv.at[column]
                ).start()

            @pl.when(j0 > 0)
            def _():
                far((me + j0) % OWNERS, i).start()

            for u in range(1, 4):
                far((me + j0 + u) % OWNERS, i).start()

    def twin(p):
        rows = got.at[stn, pl.ds(p * 32, 32)]
        return pltpu.make_async_remote_copy(
            src_ref=rows,
            dst_ref=rows,
            send_sem=twin_send.at[p],
            recv_sem=twin_recv.at[p],
            device_id={"stn": 1 - stn},
            device_id_type=MESH,
        )

    def hand_over(p):
        rows = got.at[stn, pl.ds(p * 32, 32)]
        pltpu.make_async_copy(rows, rows, far_recv.at[p]).wait()
        twin(p).start()

    hand_over((column + 3) % 4)

    @pl.loop(0, 4)
    def _(step):
        p = (column + 3 - step) % 4

        @pl.when(step < 3)
        def _():
            hand_over((column + 2 - step + 4) % 4)

        twin(p).wait_recv()
        gather_pair(p, got, wide, packed)

    correlate(stn, packed, out_ref)

    for i in range(2):
        for r in range(2):
            for offset in (1, 3, 2):
                near(i, r, offset).wait_send()

            @pl.when(block < 7)
            def _():
                halo_copy(i, r).wait_send()

    for p in range(4):
        twin(p).wait_send()
    sent = chunks.at[pl.ds(0, OWNERS - 1)]
    pltpu.make_async_copy(sent, sent, far_send).wait()


def on_device(voltages, delays):
    dma = pltpu.SemaphoreType.DMA
    f32, bf16 = jnp.float32, jnp.bfloat16
    return pl.pallas_call(
        whole_kernel,
        out_shape=jax.ShapeDtypeStruct((2, SLOW, 32, 64), f32),
        in_specs=[pl.BlockSpec(memory_space=pltpu.SMEM)] + [pl.BlockSpec(memory_space=pl.ANY)] * 4,
        out_specs=pl.BlockSpec(memory_space=pltpu.VMEM),
        scratch_shapes=[
            pltpu.VMEM((2, 8, BLOCK * CHANNELS), bf16),
            pltpu.VMEM((SLOW, TAPS, FAST), f32),
            pltpu.VMEM((SLOW, 2 * SLOW, FAST), f32),
            pltpu.VMEM((2 * FAST, 2 * FAST), f32),
            pltpu.VMEM((2, SLOW, 24, FAST), f32),
            pltpu.VMEM((2, 2 * SLOW, FAST), f32),
            pltpu.VMEM((2, 2 * FAST, 2 * FAST), bf16),
            pltpu.VMEM((2, 8 * BLOCK, FAST), f32),
            pltpu.VMEM((GROUP, 2, 2, BLOCK, CHANNELS), bf16),
            pltpu.VMEM((GROUP, 2, 2, BLOCK, CHANNELS), bf16),
            pltpu.VMEM((2, 2, BLOCK, CHANNELS), bf16),
            pltpu.VMEM((OWNERS, 2, 2, 16, FAST), bf16),
            pltpu.VMEM((2, OWNERS, 2, 2, 16, FAST), bf16),
            pltpu.VMEM((2, 64, FAST), f32),
            pltpu.VMEM((2, SLOW, 64, FAST), f32),
            pltpu.VMEM((SLOW, 64, 2 * FAST), f32),
            pltpu.VMEM((2, FAST * 16, FAST), f32),
            pltpu.VMEM((2, 2, 64 * 16, FAST), f32),
            pltpu.VMEM((SLOW, FAST, 4 * FAST), bf16),
            dma((4,)),
            dma((2, 2, GROUP)),
            dma((2, 2, GROUP)),
            dma((2, 2)),
            dma((2, 2)),
            dma,
            dma((4,)),
            dma((4,)),
            dma((4,)),
        ],
        compiler_params=pltpu.CompilerParams(
            collective_id=0, has_side_effects=True, vmem_limit_bytes=56 << 20
        ),
    )(delays, voltages, tap_blocks(), turn_blocks(), last_table())


def solution(mesh):
    return jax.shard_map(
        on_device,
        mesh=mesh,
        in_specs=(P(None, ("stn", "ct"), "tm"), P(("stn", "ct"))),
        out_specs=P(None, ("tm", "ct"), "stn", None),
        check_vma=False,
    )
```

```python
import math

import jax
import jax.numpy as jnp
import numpy as np
from jax import lax
from jax.experimental import pallas as pl
from jax.experimental.pallas import tpu as pltpu
from jax.sharding import PartitionSpec as P

CHANNELS = 4096
TAPS = 16
SLOW = 32
FAST = 128
BLOCK = 16
GROUP = 4
FRAMES = 512
OWNERS = 128
MESH = pl.DeviceIdType.MESH


def filter_table():
    length = TAPS * CHANNELS
    index = np.arange(length, dtype=np.float64)
    centred = (index - length / 2) / CHANNELS
    window = 0.5 - 0.5 * np.cos(2.0 * math.pi * index / length)
    factor = 1.0 / (48.0 * math.sqrt(CHANNELS))
    return (np.sinc(centred) * window * factor).reshape(TAPS, CHANNELS).astype(np.float32)


def tap_blocks():
    return filter_table().reshape(TAPS, SLOW, FAST).transpose(1, 0, 2)


def turn_blocks():
    angle = np.arange(SLOW)[:, None] * np.arange(CHANNELS)[None, :] % CHANNELS
    angle = angle * (2.0 * math.pi / CHANNELS)
    both = np.concatenate([np.cos(angle), np.sin(angle)]).astype(np.float32)
    return both.reshape(2 * SLOW, SLOW, FAST).transpose(1, 0, 2)


def last_table():
    angle = np.arange(FAST)[:, None] * np.arange(FAST)[None, :] % FAST * (2.0 * math.pi / FAST)
    cosine, sine = np.cos(angle), np.sin(angle)
    upper = np.concatenate([cosine, sine], axis=1)
    lower = np.concatenate([-sine, cosine], axis=1)
    return np.concatenate([upper, lower], axis=0).astype(np.float32)


def fft(xs):
    n = len(xs)
    if n == 1:
        return xs
    even, odd = fft(xs[0::2]), fft(xs[1::2])
    low, high = [], []
    for k in range(n // 2):
        re, im = odd[k]
        if k == 0:
            tr, ti = re, im
        elif 4 * k == n:
            tr, ti = im, -re
        elif 8 * k == n:
            s = math.sqrt(0.5)
            tr, ti = (re + im) * s, (im - re) * s
        elif 8 * k == 3 * n:
            s = math.sqrt(0.5)
            tr, ti = (im - re) * s, (im + re) * (-s)
        else:
            c, s = math.cos(2 * math.pi * k / n), math.sin(2 * math.pi * k / n)
            tr, ti = re * c + im * s, im * c - re * s
        er, ei = even[k]
        low.append((er + tr, ei + ti))
        high.append((er - tr, ei - ti))
    return low + high


def split_inputs(r, voltages, spread, pieces):
    @pl.loop(0, SLOW)
    def _(b):
        lanes = pl.ds(pl.multiple_of(b * FAST, FAST), FAST)
        slot = b % 2
        for f in range(BLOCK):
            there = pl.ds(pl.multiple_of(f * CHANNELS + b * FAST, FAST), FAST)
            spread[slot, pl.ds(f, 8, stride=BLOCK), :] = voltages[r, :, there].astype(jnp.float32)
        for i in range(8):
            rows = spread[slot, BLOCK * i : BLOCK * i + BLOCK, :]
            pieces[i // 2, i % 2, r, :, lanes] = rows.astype(jnp.bfloat16)


def delayed_tables(i, delay, tap_ref, turn_all, last_all, taps_ref, turn_ref, last_ref):
    high, low = delay >> 7, delay & 127
    lane = lax.broadcasted_iota(jnp.int32, (1, FAST), 1)
    same = lane < FAST - low
    shift = (FAST - low) & 127

    def ahead(table, b):
        first = pltpu.roll(table[(b + high) & 31], shift, 1)
        second = pltpu.roll(table[(b + high + 1) & 31], shift, 1)
        return jnp.where(same, first, second)

    @pl.loop(0, SLOW)
    def _(b):
        rolled = ahead(tap_ref, b)
        carry = lane + b * FAST + delay >= CHANNELS
        taps_ref[i, b, 0:TAPS, :] = jnp.where(carry, 0.0, rolled)
        taps_ref[i, b, TAPS : TAPS + 8, :] = jnp.zeros((8, FAST), jnp.float32)
        taps_ref[i, b, 1 : TAPS + 1, :] += jnp.where(carry, rolled, 0.0)

    turn_ref[i] = ahead(turn_all, 0)

    @pl.loop(0, 8)
    def _(g):
        rows = pl.ds(pl.multiple_of(g * 32, 32), 32)
        for part in range(2):
            lanes = slice(part * FAST, part * FAST + FAST)
            last_ref[i, rows, lanes] = pltpu.roll(last_all[rows, lanes], shift, 1).astype(jnp.bfloat16)


def filter_frames(i, own, halo, taps_ref, xs, branch, first):
    octets = range(2) if first else range(2, 8)
    base = BLOCK if first else 0

    @pl.loop(0, SLOW)
    def _(b):
        lanes = pl.ds(pl.multiple_of(b * FAST, FAST), FAST)
        taps = [jnp.broadcast_to(taps_ref[i, b, k : k + 1, :], (8, FAST)) for k in range(TAPS + 1)]
        for r in range(2):
            if first:
                xs[r, 0:BLOCK, :] = halo[i, r, :, lanes].astype(jnp.float32)
                xs[r, BLOCK : 2 * BLOCK, :] = own[0, i, r, :, lanes].astype(jnp.float32)
            else:
                for g in range(GROUP):
                    xs[r, BLOCK * g : BLOCK * g + BLOCK, :] = own[g, i, r, :, lanes].astype(
                        jnp.float32
                    )
        for r in range(2):
            total = {}
            for s in range(8 * octets[0] - TAPS, 8 * octets[-1] + 1):
                window = xs[r, base + s : base + s + 8, :]
                for o in octets:
                    k = 8 * o - s
                    if 0 <= k <= TAPS:
                        term = taps[k] * window
                        total[o] = total[o] + term if o in total else term
                    if k == 0:
                        branch[r, b, 8 * o : 8 * o + 8, :] = total[o]


def slow_transform(i, turn_ref, branch, inner, first):
    @pl.loop(*((0, 2) if first else (2, 8)))
    def _(o):
        rows = pl.ds(pl.multiple_of(o * 8, 8), 8)
        points = [(branch[0, b, rows, :], branch[1, b, rows, :]) for b in range(SLOW)]
        for k, (re, im) in enumerate(fft(points)):
            c = jnp.broadcast_to(turn_ref[i, k : k + 1, :], (8, FAST))
            s = jnp.broadcast_to(turn_ref[i, SLOW + k : SLOW + k + 1, :], (8, FAST))
            inner[k, rows, 0:FAST] = re * c + im * s
            inner[k, rows, FAST : 2 * FAST] = im * c - re * s


def fast_transform(i, last_ref, inner, flat):
    @pl.loop(0, 8)
    def _(g):
        points = inner[pl.ds(g * 4, 4), :, :].reshape(4 * 64, 2 * FAST).astype(jnp.bfloat16)
        result = lax.dot_general(
            last_ref[i], points, (((1,), (1,)), ((), ())), preferred_element_type=jnp.float32
        )
        for r in range(2):
            for t in range(2):
                for l in range(16):
                    piece = result[r * FAST + 8 * l : r * FAST + 8 * l + 8, t * FAST : t * FAST + FAST]
                    flat[r, pl.ds(l * 128 + g * 2 + t, 8, stride=16), :] = piece


def widen(pair, got, wide):
    @pl.loop(0, 4)
    def _(step):
        t = step // 2
        stn = step % 2
        for ct in range(4):
            for y in range(4):
                for i in range(2):
                    for r in range(2):
                        row = stn * 32 + (ct * 4 + y) * 2 + i
                        source = (pair * 2 + t) * 16 + y * 4 + ct
                        place = pl.ds(pl.multiple_of(row * 16, 16), 16)
                        wide[t, r, place, :] = got[stn, source, i, r, :, :].astype(jnp.float32)


def reorder(j, lanes, wide, packed):
    low = lax.broadcasted_iota(jnp.int32, (8, FAST), 1) < 64
    for r in range(2):
        for g in range(4):
            even, odd = [], []
            for h in range(2):
                rows = pl.ds((g * 16 + h * 8) * 16 + j, 8, stride=16)
                a, b = wide[0, r, rows, :], wide[1, r, rows, :]
                crossed = pltpu.roll(jnp.where(low, b, a), 64, 1)
                even.append(jnp.where(low, a, crossed))
                odd.append(jnp.where(low, crossed, b))
            place = slice(r * 64 + g * 16, r * 64 + g * 16 + 16)
            packed[2 * j, place, lanes] = jnp.concatenate(even, axis=0).astype(jnp.bfloat16)
            packed[2 * j + 1, place, lanes] = jnp.concatenate(odd, axis=0).astype(jnp.bfloat16)


def products(k, mine, lanes, packed):
    left = jnp.concatenate(
        [packed[k, pl.ds(pl.multiple_of(r * 64 + mine * 32, 32), 32), lanes] for r in range(2)], axis=0
    )
    return lax.dot_general(
        left, packed[k, :, lanes], (((1,), (1,)), ((), ())), preferred_element_type=jnp.float32
    )


def first_three(mine, packed, sums):
    @pl.loop(0, SLOW, step=4)
    def _(k0):
        for u in range(4):
            sums[k0 + u] = products(k0 + u, mine, slice(0, 3 * FAST), packed)


def last_one(mine, wide, packed, sums, out_ref):
    lanes = slice(3 * FAST, 4 * FAST)

    @pl.loop(0, 16, step=4)
    def _(j0):
        for u in range(4):
            reorder(j0 + u, lanes, wide, packed)
        for u in range(8):
            k = 2 * j0 + u
            grid = sums[k] + products(k, mine, lanes, packed)
            out_ref[0, k, :, :] = (grid[0:32, 0:64] + grid[32:64, 64:128]) * (1.0 / FRAMES)
            out_ref[1, k, :, :] = (grid[32:64, 0:64] - grid[0:32, 64:128]) * (1.0 / FRAMES)


def whole_kernel(
    delays,
    voltages_hbm,
    tap_hbm,
    turn_hbm,
    last_hbm,
    out_ref,
    voltages,
    tap_all,
    turn_all,
    last_all,
    taps_ref,
    turn_ref,
    last_ref,
    spread,
    pieces,
    own,
    halo,
    chunks,
    got,
    xs,
    branch,
    inner,
    flat,
    wide,
    packed,
    sums,
    load_sem,
    all_sem,
    near_send,
    near_recv,
    halo_send,
    halo_recv,
    far_send,
    far_recv,
    twin_send,
    twin_recv,
):
    tm, ct, stn = lax.axis_index("tm"), lax.axis_index("ct"), lax.axis_index("stn")
    me = tm * 4 + ct
    y, block, column = tm % 4, tm // 4, tm // 8

    loads = [
        pltpu.make_async_copy(voltages_hbm.at[0], voltages.at[0], load_sem.at[0]),
        pltpu.make_async_copy(voltages_hbm.at[1], voltages.at[1], load_sem.at[1]),
        pltpu.make_async_copy(tap_hbm, tap_all, load_sem.at[2]),
        pltpu.make_async_copy(turn_hbm, turn_all, load_sem.at[3]),
        pltpu.make_async_copy(last_hbm, last_all, load_sem.at[4]),
    ]
    for load in loads:
        load.start()

    def along_y(offset):
        return {"tm": block * 4 + (y + offset) % 4, "ct": ct}

    def along_z(offset):
        z = ((block % 2) * 4 + ct + offset) % 8
        return {"tm": column * 8 + (z // 4) * 4 + y, "ct": z % 4}

    def along_x(offset):
        return {"tm": (tm + 8 * offset) % 32, "ct": ct}

    diagonal = {"tm": (tm + jnp.where(block % 2 == 0, 28, 4)) % 32, "ct": ct}
    greeted = [along_y(o) for o in range(1, 4)] + [{"stn": 1 - stn}, diagonal]
    greeted += [along_z(o) for o in range(1, 8)] + [along_x(o) for o in range(1, 4)]
    barrier = pltpu.get_barrier_semaphore()
    for other in greeted:
        pl.semaphore_signal(barrier, inc=1, device_id=other, device_id_type=MESH)

    @pl.when(block == 0)
    def _():
        halo[...] = jnp.zeros_like(halo)

    loads[0].wait()
    split_inputs(0, voltages, spread, pieces)
    pl.semaphore_wait(barrier, len(greeted))

    def near(i, r, offset):
        other = (y + offset) % GROUP
        return pltpu.make_async_remote_copy(
            src_ref=pieces.at[other, i, r],
            dst_ref=own.at[y, i, r],
            send_sem=near_send.at[i, r, offset],
            recv_sem=near_recv.at[i, r, y],
            device_id={"tm": block * 4 + other},
            device_id_type=MESH,
        )

    def near_arrival(i, r, source):
        return pltpu.make_async_copy(
            pieces.at[0, i, r], own.at[source, i, r], near_recv.at[i, r, source]
        )

    def halo_copy(i, r):
        return pltpu.make_async_remote_copy(
            src_ref=own.at[GROUP - 1, i, r],
            dst_ref=halo.at[i, r],
            send_sem=halo_send.at[i, r],
            recv_sem=halo_recv.at[i, r],
            device_id={"tm": (tm + GROUP) % 32},
            device_id_type=MESH,
        )

    def pass_on(i):
        for r in range(2):
            near_arrival(i, r, GROUP - 1).wait()

            @pl.when(block < 7)
            def _():
                halo_copy(i, r).start()

    def exchange(i, r):
        pltpu.make_async_copy(pieces.at[y, i, r], own.at[y, i, r], near_recv.at[i, r, y]).start()
        for offset in (1, 3, 2):
            near(i, r, offset).start()

    exchange(0, 0)
    loads[1].wait()
    split_inputs(1, voltages, spread, pieces)
    exchange(0, 1)
    exchange(1, 0)
    exchange(1, 1)

    for offset in range(1, 8):
        pl.semaphore_signal(all_sem.at[0], inc=1, device_id=along_z(offset), device_id_type=MESH)
    pl.semaphore_wait(all_sem.at[0], 7)
    for offset in range(1, 4):
        pl.semaphore_signal(all_sem.at[1], inc=1, device_id=along_y(offset), device_id_type=MESH)

    for load in loads[2:]:
        load.wait()
    for i in range(2):
        delayed_tables(
            i, delays[2 * y + i], tap_all, turn_all, last_all, taps_ref, turn_ref, last_ref
        )
        if i == 0:
            pass_on(0)

    def far(l, i):
        return pltpu.make_async_remote_copy(
            src_ref=chunks.at[l, i],
            dst_ref=got.at[stn, me, i],
            send_sem=far_send,
            recv_sem=far_recv.at[column],
            device_id={"tm": l // 4, "ct": l % 4},
            device_id_type=MESH,
        )

    @pl.loop(0, 2)
    def _(i):
        for r in range(2):
            for source in range(GROUP - 1):
                near_arrival(i, r, source).wait()

        filter_frames(i, own, halo, taps_ref, xs, branch, False)
        slow_transform(i, turn_ref, branch, inner, False)

        @pl.when(i == 0)
        def _():
            pass_on(1)

        @pl.when(block > 0)
        def _():
            for r in range(2):
                halo_copy(i, r).wait_recv()

        filter_frames(i, own, halo, taps_ref, xs, branch, True)
        slow_transform(i, turn_ref, branch, inner, True)
        fast_transform(i, last_ref, inner, flat)

        @pl.when(i == 0)
        def _():
            pl.semaphore_wait(all_sem.at[1], 3)

        @pl.loop(0, OWNERS, step=4)
        def _(j0):
            for u in range(4):
                l = (me + j0 + u) % OWNERS
                rows = pl.ds(pl.multiple_of(l * 16, 16), 16)
                for r in range(2):
                    chunks[l, i, r, :, :] = flat[r, rows, :].astype(jnp.bfloat16)

            @pl.when(j0 == 0)
            def _():
                pltpu.make_async_copy(
                    chunks.at[me, i], got.at[stn, me, i], far_recv.at[column]
                ).start()

            @pl.when(j0 > 0)
            def _():
                far((me + j0) % OWNERS, i).start()

            for u in range(1, 4):
                far((me + j0 + u) % OWNERS, i).start()

    def twin(p):
        rows = got.at[stn, pl.ds(p * 32, 32)]
        return pltpu.make_async_remote_copy(
            src_ref=rows,
            dst_ref=rows,
            send_sem=twin_send.at[p],
            recv_sem=twin_recv.at[p],
            device_id={"stn": 1 - stn},
            device_id_type=MESH,
        )

    def hand_over(p):
        rows = got.at[stn, pl.ds(p * 32, 32)]
        pltpu.make_async_copy(rows, rows, far_recv.at[p]).wait()
        twin(p).start()

    hand_over((column + 3) % 4)

    for step in range(4):
        p = (column + 3 - step) % 4
        if step < 3:
            hand_over((column + 2 - step) % 4)
        twin(p).wait_recv()
        widen(p, got, wide)
        if step < 3:

            @pl.loop(0, 16, step=4)
            def _(j0):
                for u in range(4):
                    reorder(j0 + u, slice(step * FAST, step * FAST + FAST), wide, packed)

        if step == 2:
            first_three(stn, packed, sums)
    last_one(stn, wide, packed, sums, out_ref)

    for i in range(2):
        for r in range(2):
            for offset in (1, 3, 2):
                near(i, r, offset).wait_send()

            @pl.when(block < 7)
            def _():
                halo_copy(i, r).wait_send()

    for p in range(4):
        twin(p).wait_send()
    sent = chunks.at[pl.ds(0, OWNERS - 1)]
    pltpu.make_async_copy(sent, sent, far_send).wait()


def on_device(voltages, delays):
    dma = pltpu.SemaphoreType.DMA
    f32, bf16 = jnp.float32, jnp.bfloat16
    return pl.pallas_call(
        whole_kernel,
        out_shape=jax.ShapeDtypeStruct((2, SLOW, 32, 64), f32),
        in_specs=[pl.BlockSpec(memory_space=pltpu.SMEM)] + [pl.BlockSpec(memory_space=pl.ANY)] * 4,
        out_specs=pl.BlockSpec(memory_space=pltpu.VMEM),
        scratch_shapes=[
            pltpu.VMEM((2, 8, BLOCK * CHANNELS), bf16),
            pltpu.VMEM((SLOW, TAPS, FAST), f32),
            pltpu.VMEM((SLOW, 2 * SLOW, FAST), f32),
            pltpu.VMEM((2 * FAST, 2 * FAST), f32),
            pltpu.VMEM((2, SLOW, 24, FAST), f32),
            pltpu.VMEM((2, 2 * SLOW, FAST), f32),
            pltpu.VMEM((2, 2 * FAST, 2 * FAST), bf16),
            pltpu.VMEM((2, 8 * BLOCK, FAST), f32),
            pltpu.VMEM((GROUP, 2, 2, BLOCK, CHANNELS), bf16),
            pltpu.VMEM((GROUP, 2, 2, BLOCK, CHANNELS), bf16),
            pltpu.VMEM((2, 2, BLOCK, CHANNELS), bf16),
            pltpu.VMEM((OWNERS, 2, 2, 16, FAST), bf16),
            pltpu.VMEM((2, OWNERS, 2, 2, 16, FAST), bf16),
            pltpu.VMEM((2, 64, FAST), f32),
            pltpu.VMEM((2, SLOW, 64, FAST), f32),
            pltpu.VMEM((SLOW, 64, 2 * FAST), f32),
            pltpu.VMEM((2, FAST * 16, FAST), f32),
            pltpu.VMEM((2, 2, 64 * 16, FAST), f32),
            pltpu.VMEM((SLOW, FAST, 4 * FAST), bf16),
            pltpu.VMEM((SLOW, 64, FAST), f32),
            dma((5,)),
            pltpu.SemaphoreType.REGULAR((2,)),
            dma((2, 2, GROUP)),
            dma((2, 2, GROUP)),
            dma((2, 2)),
            dma((2, 2)),
            dma,
            dma((4,)),
            dma((4,)),
            dma((4,)),
        ],
        compiler_params=pltpu.CompilerParams(
            collective_id=0, has_side_effects=True, vmem_limit_bytes=56 << 20
        ),
    )(delays, voltages, tap_blocks(), turn_blocks(), last_table())


def solution(mesh):
    return jax.shard_map(
        on_device,
        mesh=mesh,
        in_specs=(P(None, ("stn", "ct"), "tm"), P(("stn", "ct"))),
        out_specs=P(None, ("tm", "ct"), "stn", None),
        check_vma=False,
    )
```

```python
import math

import jax
import jax.numpy as jnp
import numpy as np
from jax import lax
from jax.experimental import pallas as pl
from jax.experimental.pallas import tpu as pltpu
from jax.sharding import PartitionSpec as P

CHANNELS = 4096
TAPS = 16
SLOW = 32
FAST = 128
BLOCK = 16
GROUP = 4
FRAMES = 512
OWNERS = 128
MESH = pl.DeviceIdType.MESH


def filter_table():
    length = TAPS * CHANNELS
    index = np.arange(length, dtype=np.float64)
    centred = (index - length / 2) / CHANNELS
    window = 0.5 - 0.5 * np.cos(2.0 * math.pi * index / length)
    factor = 1.0 / (48.0 * math.sqrt(CHANNELS))
    return (np.sinc(centred) * window * factor).reshape(TAPS, CHANNELS).astype(np.float32)


def tap_blocks():
    return filter_table().reshape(TAPS, SLOW, FAST).transpose(1, 0, 2)


def turn_blocks():
    angle = np.arange(SLOW)[:, None] * np.arange(CHANNELS)[None, :] % CHANNELS
    angle = angle * (2.0 * math.pi / CHANNELS)
    both = np.concatenate([np.cos(angle), np.sin(angle)]).astype(np.float32)
    return both.reshape(2 * SLOW, SLOW, FAST).transpose(1, 0, 2)


def last_table():
    angle = np.arange(FAST)[:, None] * np.arange(FAST)[None, :] % FAST * (2.0 * math.pi / FAST)
    cosine, sine = np.cos(angle), np.sin(angle)
    upper = np.concatenate([cosine, sine], axis=1)
    lower = np.concatenate([-sine, cosine], axis=1)
    return np.concatenate([upper, lower], axis=0).astype(np.float32)


def fft(xs):
    n = len(xs)
    if n == 1:
        return xs
    even, odd = fft(xs[0::2]), fft(xs[1::2])
    low, high = [], []
    for k in range(n // 2):
        re, im = odd[k]
        if k == 0:
            tr, ti = re, im
        elif 4 * k == n:
            tr, ti = im, -re
        elif 8 * k == n:
            s = math.sqrt(0.5)
            tr, ti = (re + im) * s, (im - re) * s
        elif 8 * k == 3 * n:
            s = math.sqrt(0.5)
            tr, ti = (im - re) * s, (im + re) * (-s)
        else:
            c, s = math.cos(2 * math.pi * k / n), math.sin(2 * math.pi * k / n)
            tr, ti = re * c + im * s, im * c - re * s
        er, ei = even[k]
        low.append((er + tr, ei + ti))
        high.append((er - tr, ei - ti))
    return low + high


def split_inputs(r, voltages, spread, pieces):
    @pl.loop(0, SLOW)
    def _(b):
        lanes = pl.ds(pl.multiple_of(b * FAST, FAST), FAST)
        slot = b % 2
        for f in range(BLOCK):
            there = pl.ds(pl.multiple_of(f * CHANNELS + b * FAST, FAST), FAST)
            spread[slot, pl.ds(f, 8, stride=BLOCK), :] = voltages[r, :, there].astype(jnp.float32)
        for i in range(8):
            rows = spread[slot, BLOCK * i : BLOCK * i + BLOCK, :]
            pieces[i // 2, i % 2, r, :, lanes] = rows.astype(jnp.bfloat16)


def delayed_tables(i, delay, tap_ref, turn_all, last_all, taps_ref, turn_ref, last_ref):
    high, low = delay >> 7, delay & 127
    lane = lax.broadcasted_iota(jnp.int32, (1, FAST), 1)
    same = lane < FAST - low
    shift = (FAST - low) & 127

    def ahead(table, b):
        first = pltpu.roll(table[(b + high) & 31], shift, 1)
        second = pltpu.roll(table[(b + high + 1) & 31], shift, 1)
        return jnp.where(same, first, second)

    @pl.loop(0, SLOW)
    def _(b):
        rolled = ahead(tap_ref, b)
        carry = lane + b * FAST + delay >= CHANNELS
        taps_ref[i, b, 0:TAPS, :] = jnp.where(carry, 0.0, rolled)
        taps_ref[i, b, TAPS : TAPS + 8, :] = jnp.zeros((8, FAST), jnp.float32)
        taps_ref[i, b, 1 : TAPS + 1, :] += jnp.where(carry, rolled, 0.0)

    turn_ref[i] = ahead(turn_all, 0)

    @pl.loop(0, 8)
    def _(g):
        rows = pl.ds(pl.multiple_of(g * 32, 32), 32)
        for part in range(2):
            lanes = slice(part * FAST, part * FAST + FAST)
            last_ref[i, rows, lanes] = pltpu.roll(last_all[rows, lanes], shift, 1).astype(jnp.bfloat16)


def filter_frames(i, own, halo, taps_ref, xs, branch, first):
    octets = range(2) if first else range(2, 8)
    base = BLOCK if first else 0

    @pl.loop(0, SLOW)
    def _(b):
        lanes = pl.ds(pl.multiple_of(b * FAST, FAST), FAST)
        taps = [jnp.broadcast_to(taps_ref[i, b, k : k + 1, :], (8, FAST)) for k in range(TAPS + 1)]
        for r in range(2):
            if first:
                xs[r, 0:BLOCK, :] = halo[i, r, :, lanes].astype(jnp.float32)
                xs[r, BLOCK : 2 * BLOCK, :] = own[0, i, r, :, lanes].astype(jnp.float32)
            else:
                for g in range(GROUP):
                    xs[r, BLOCK * g : BLOCK * g + BLOCK, :] = own[g, i, r, :, lanes].astype(
                        jnp.float32
                    )
        for r in range(2):
            total = {}
            for s in range(8 * octets[0] - TAPS, 8 * octets[-1] + 1):
                window = xs[r, base + s : base + s + 8, :]
                for o in octets:
                    k = 8 * o - s
                    if 0 <= k <= TAPS:
                        term = taps[k] * window
                        total[o] = total[o] + term if o in total else term
                    if k == 0:
                        branch[r, b, 8 * o : 8 * o + 8, :] = total[o]


def slow_transform(i, turn_ref, branch, inner, first):
    @pl.loop(*((0, 2) if first else (2, 8)))
    def _(o):
        rows = pl.ds(pl.multiple_of(o * 8, 8), 8)
        points = [(branch[0, b, rows, :], branch[1, b, rows, :]) for b in range(SLOW)]
        for k, (re, im) in enumerate(fft(points)):
            c = jnp.broadcast_to(turn_ref[i, k : k + 1, :], (8, FAST))
            s = jnp.broadcast_to(turn_ref[i, SLOW + k : SLOW + k + 1, :], (8, FAST))
            inner[k, rows, 0:FAST] = re * c + im * s
            inner[k, rows, FAST : 2 * FAST] = im * c - re * s


def fast_transform(i, last_ref, inner, flat):
    @pl.loop(0, 8)
    def _(g):
        points = inner[pl.ds(g * 4, 4), :, :].reshape(4 * 64, 2 * FAST).astype(jnp.bfloat16)
        result = lax.dot_general(
            last_ref[i], points, (((1,), (1,)), ((), ())), preferred_element_type=jnp.float32
        )
        for r in range(2):
            for t in range(2):
                for l in range(16):
                    piece = result[r * FAST + 8 * l : r * FAST + 8 * l + 8, t * FAST : t * FAST + FAST]
                    flat[r, pl.ds(l * 128 + g * 2 + t, 8, stride=16), :] = piece


def widen(block, got, wide):
    @pl.loop(0, 2)
    def _(stn):
        for ct in range(4):
            for y in range(4):
                for i in range(2):
                    for r in range(2):
                        row = stn * 32 + (ct * 4 + y) * 2 + i
                        place = pl.ds(pl.multiple_of(row * 16, 16), 16)
                        wide[r, place, :] = got[stn, block * 16 + y * 4 + ct, i, r, :, :].astype(
                            jnp.float32
                        )


def reorder(j, lanes, wide, packed):
    for r in range(2):
        for g in range(4):
            rows = [wide[r, pl.ds((g * 16 + h * 8) * 16 + j, 8, stride=16), :] for h in range(2)]
            place = slice(r * 64 + g * 16, r * 64 + g * 16 + 16)
            packed[j, place, lanes] = jnp.concatenate(rows, axis=0).astype(jnp.bfloat16)


def reorder_all(step, wide, packed):
    lanes = pl.ds(pl.multiple_of(step * FAST, FAST), FAST)

    @pl.loop(0, 16, step=4)
    def _(j0):
        for u in range(4):
            reorder(j0 + u, lanes, wide, packed)


def products(j, mine, begin, end, packed):
    lanes = slice(begin * FAST, end * FAST)
    shape = (64, (end - begin) * FAST)
    even = (lax.broadcasted_iota(jnp.int32, shape, 1) % FAST < 64).astype(jnp.float32)
    even = even.astype(jnp.bfloat16)
    left = jnp.concatenate(
        [packed[j, pl.ds(pl.multiple_of(r * 64 + mine * 32, 32), 32), lanes] for r in range(2)], axis=0
    )
    left = jnp.concatenate([left * even, left * (1 - even)], axis=0)
    return lax.dot_general(
        left, packed[j, :, lanes], (((1,), (1,)), ((), ())), preferred_element_type=jnp.float32
    )


def first_six(mine, packed, sums):
    @pl.loop(0, 16, step=2)
    def _(j0):
        for u in range(2):
            sums[j0 + u] = products(j0 + u, mine, 0, 6, packed)


def last_two(mine, wide, packed, sums, out_ref):
    @pl.loop(0, 16, step=4)
    def _(j0):
        for u in range(4):
            reorder(j0 + u, slice(7 * FAST, 8 * FAST), wide, packed)
        for u in range(4):
            j = j0 + u
            both = sums[j] + products(j, mine, 6, 8, packed)
            for odd in range(2):
                grid = both[64 * odd : 64 * odd + 64]
                k = 2 * j + odd
                out_ref[0, k, :, :] = (grid[0:32, 0:64] + grid[32:64, 64:128]) * (1.0 / FRAMES)
                out_ref[1, k, :, :] = (grid[32:64, 0:64] - grid[0:32, 64:128]) * (1.0 / FRAMES)


def whole_kernel(
    delays,
    voltages_hbm,
    tap_hbm,
    turn_hbm,
    last_hbm,
    out_ref,
    voltages,
    tap_all,
    turn_all,
    last_all,
    taps_ref,
    turn_ref,
    last_ref,
    spread,
    pieces,
    own,
    halo,
    chunks,
    got,
    xs,
    branch,
    inner,
    flat,
    wide,
    packed,
    sums,
    load_sem,
    all_sem,
    near_send,
    near_recv,
    halo_send,
    halo_recv,
    far_send,
    far_recv,
    twin_send,
    twin_recv,
):
    tm, ct, stn = lax.axis_index("tm"), lax.axis_index("ct"), lax.axis_index("stn")
    me = tm * 4 + ct
    y, block, column = tm % 4, tm // 4, tm // 8

    loads = [
        pltpu.make_async_copy(voltages_hbm.at[0], voltages.at[0], load_sem.at[0]),
        pltpu.make_async_copy(voltages_hbm.at[1], voltages.at[1], load_sem.at[1]),
        pltpu.make_async_copy(tap_hbm, tap_all, load_sem.at[2]),
        pltpu.make_async_copy(turn_hbm, turn_all, load_sem.at[3]),
        pltpu.make_async_copy(last_hbm, last_all, load_sem.at[4]),
    ]
    for load in loads:
        load.start()

    def along_y(offset):
        return {"tm": block * 4 + (y + offset) % 4, "ct": ct}

    def along_z(offset):
        z = ((block % 2) * 4 + ct + offset) % 8
        return {"tm": column * 8 + (z // 4) * 4 + y, "ct": z % 4}

    def along_x(offset):
        return {"tm": (tm + 8 * offset) % 32, "ct": ct}

    diagonal = {"tm": (tm + jnp.where(block % 2 == 0, 28, 4)) % 32, "ct": ct}
    greeted = [along_y(o) for o in range(1, 4)] + [{"stn": 1 - stn}, diagonal]
    greeted += [along_z(o) for o in range(1, 8)] + [along_x(o) for o in range(1, 4)]
    barrier = pltpu.get_barrier_semaphore()
    for other in greeted:
        pl.semaphore_signal(barrier, inc=1, device_id=other, device_id_type=MESH)

    @pl.when(block == 0)
    def _():
        halo[...] = jnp.zeros_like(halo)

    loads[0].wait()
    split_inputs(0, voltages, spread, pieces)
    pl.semaphore_wait(barrier, len(greeted))

    def near(i, r, offset):
        other = (y + offset) % GROUP
        return pltpu.make_async_remote_copy(
            src_ref=pieces.at[other, i, r],
            dst_ref=own.at[y, i, r],
            send_sem=near_send.at[i, r, offset],
            recv_sem=near_recv.at[i, r, y],
            device_id={"tm": block * 4 + other},
            device_id_type=MESH,
        )

    def near_arrival(i, r, source):
        return pltpu.make_async_copy(
            pieces.at[0, i, r], own.at[source, i, r], near_recv.at[i, r, source]
        )

    def halo_copy(i, r):
        return pltpu.make_async_remote_copy(
            src_ref=own.at[GROUP - 1, i, r],
            dst_ref=halo.at[i, r],
            send_sem=halo_send.at[i, r],
            recv_sem=halo_recv.at[i, r],
            device_id={"tm": (tm + GROUP) % 32},
            device_id_type=MESH,
        )

    def pass_on(i):
        for r in range(2):
            near_arrival(i, r, GROUP - 1).wait()

            @pl.when(block < 7)
            def _():
                halo_copy(i, r).start()

    def exchange(i, r):
        pltpu.make_async_copy(pieces.at[y, i, r], own.at[y, i, r], near_recv.at[i, r, y]).start()
        for offset in (1, 3, 2):
            near(i, r, offset).start()

    exchange(0, 0)
    loads[1].wait()
    split_inputs(1, voltages, spread, pieces)
    exchange(0, 1)

    for offset in range(1, 8):
        pl.semaphore_signal(all_sem.at[0], inc=1, device_id=along_z(offset), device_id_type=MESH)
    pl.semaphore_wait(all_sem.at[0], 7)
    for offset in range(1, 4):
        pl.semaphore_signal(all_sem.at[1], inc=1, device_id=along_y(offset), device_id_type=MESH)

    for load in loads[2:]:
        load.wait()
    for i in range(2):
        delayed_tables(
            i, delays[2 * y + i], tap_all, turn_all, last_all, taps_ref, turn_ref, last_ref
        )
        if i == 0:
            pass_on(0)

    def far(l, i):
        return pltpu.make_async_remote_copy(
            src_ref=chunks.at[l, i],
            dst_ref=got.at[stn, me, i],
            send_sem=far_send,
            recv_sem=far_recv.at[block],
            device_id={"tm": l // 4, "ct": l % 4},
            device_id_type=MESH,
        )

    @pl.loop(0, 2)
    def _(i):
        for r in range(2):
            for source in range(GROUP - 1):
                near_arrival(i, r, source).wait()

            @pl.when(i == 0)
            def _():
                exchange(1, r)

        filter_frames(i, own, halo, taps_ref, xs, branch, False)
        slow_transform(i, turn_ref, branch, inner, False)

        @pl.when(i == 0)
        def _():
            pass_on(1)

        @pl.when(block > 0)
        def _():
            for r in range(2):
                halo_copy(i, r).wait_recv()

        filter_frames(i, own, halo, taps_ref, xs, branch, True)
        slow_transform(i, turn_ref, branch, inner, True)
        fast_transform(i, last_ref, inner, flat)

        @pl.when(i == 0)
        def _():
            pl.semaphore_wait(all_sem.at[1], 3)

        @pl.loop(0, OWNERS, step=4)
        def _(j0):
            for u in range(4):
                l = (me + j0 + u) % OWNERS
                rows = pl.ds(pl.multiple_of(l * 16, 16), 16)
                for r in range(2):
                    chunks[l, i, r, :, :] = flat[r, rows, :].astype(jnp.bfloat16)

            @pl.when(j0 == 0)
            def _():
                pltpu.make_async_copy(
                    chunks.at[me, i], got.at[stn, me, i], far_recv.at[block]
                ).start()

            @pl.when(j0 > 0)
            def _():
                far((me + j0) % OWNERS, i).start()

            for u in range(1, 4):
                far((me + j0 + u) % OWNERS, i).start()

    def twin(p):
        rows = got.at[stn, pl.ds(p * 16, 16)]
        return pltpu.make_async_remote_copy(
            src_ref=rows,
            dst_ref=rows,
            send_sem=twin_send.at[p],
            recv_sem=twin_recv.at[p],
            device_id={"stn": 1 - stn},
            device_id_type=MESH,
        )

    def turn(step):
        return (block + 7 - step) % 8

    def hand_over(step):
        rows = got.at[stn, pl.ds(turn(step) * 16, 16)]
        pltpu.make_async_copy(rows, rows, far_recv.at[turn(step)]).wait()
        twin(turn(step)).start()

    def take(step):
        twin(turn(step)).wait_recv()
        widen(turn(step), got, wide)

    hand_over(0)

    @pl.loop(0, 6)
    def _(step):
        @pl.when(step < 5)
        def _():
            hand_over(step + 1)

        take(step)
        reorder_all(step, wide, packed)

    first_six(stn, packed, sums)
    hand_over(6)
    hand_over(7)
    take(6)
    reorder_all(6, wide, packed)
    take(7)
    last_two(stn, wide, packed, sums, out_ref)

    for i in range(2):
        for r in range(2):
            for offset in (1, 3, 2):
                near(i, r, offset).wait_send()

            @pl.when(block < 7)
            def _():
                halo_copy(i, r).wait_send()

    for p in range(8):
        twin(p).wait_send()
    sent = chunks.at[pl.ds(0, OWNERS - 1)]
    pltpu.make_async_copy(sent, sent, far_send).wait()


def on_device(voltages, delays):
    dma = pltpu.SemaphoreType.DMA
    f32, bf16 = jnp.float32, jnp.bfloat16
    return pl.pallas_call(
        whole_kernel,
        out_shape=jax.ShapeDtypeStruct((2, SLOW, 32, 64), f32),
        in_specs=[pl.BlockSpec(memory_space=pltpu.SMEM)] + [pl.BlockSpec(memory_space=pl.ANY)] * 4,
        out_specs=pl.BlockSpec(memory_space=pltpu.VMEM),
        scratch_shapes=[
            pltpu.VMEM((2, 8, BLOCK * CHANNELS), bf16),
            pltpu.VMEM((SLOW, TAPS, FAST), f32),
            pltpu.VMEM((SLOW, 2 * SLOW, FAST), f32),
            pltpu.VMEM((2 * FAST, 2 * FAST), f32),
            pltpu.VMEM((2, SLOW, 24, FAST), f32),
            pltpu.VMEM((2, 2 * SLOW, FAST), f32),
            pltpu.VMEM((2, 2 * FAST, 2 * FAST), bf16),
            pltpu.VMEM((2, 8 * BLOCK, FAST), f32),
            pltpu.VMEM((GROUP, 2, 2, BLOCK, CHANNELS), bf16),
            pltpu.VMEM((GROUP, 2, 2, BLOCK, CHANNELS), bf16),
            pltpu.VMEM((2, 2, BLOCK, CHANNELS), bf16),
            pltpu.VMEM((OWNERS, 2, 2, 16, FAST), bf16),
            pltpu.VMEM((2, OWNERS, 2, 2, 16, FAST), bf16),
            pltpu.VMEM((2, 64, FAST), f32),
            pltpu.VMEM((2, SLOW, 64, FAST), f32),
            pltpu.VMEM((SLOW, 64, 2 * FAST), f32),
            pltpu.VMEM((2, FAST * 16, FAST), f32),
            pltpu.VMEM((2, 64 * 16, FAST), f32),
            pltpu.VMEM((16, FAST, 8 * FAST), bf16),
            pltpu.VMEM((16, FAST, FAST), f32),
            dma((5,)),
            pltpu.SemaphoreType.REGULAR((2,)),
            dma((2, 2, GROUP)),
            dma((2, 2, GROUP)),
            dma((2, 2)),
            dma((2, 2)),
            dma,
            dma((8,)),
            dma((8,)),
            dma((8,)),
        ],
        compiler_params=pltpu.CompilerParams(
            collective_id=0, has_side_effects=True, vmem_limit_bytes=56 << 20
        ),
    )(delays, voltages, tap_blocks(), turn_blocks(), last_table())


def solution(mesh):
    return jax.shard_map(
        on_device,
        mesh=mesh,
        in_specs=(P(None, ("stn", "ct"), "tm"), P(("stn", "ct"))),
        out_specs=P(None, ("tm", "ct"), "stn", None),
        check_vma=False,
    )
```

```python
import math

import jax
import jax.numpy as jnp
import numpy as np
from jax import lax
from jax.experimental import pallas as pl
from jax.experimental.pallas import tpu as pltpu
from jax.sharding import PartitionSpec as P

CHANNELS = 4096
TAPS = 16
SLOW = 32
FAST = 128
BLOCK = 16
GROUP = 4
FRAMES = 512
OWNERS = 128
MESH = pl.DeviceIdType.MESH


def filter_table():
    length = TAPS * CHANNELS
    index = np.arange(length, dtype=np.float64)
    centred = (index - length / 2) / CHANNELS
    window = 0.5 - 0.5 * np.cos(2.0 * math.pi * index / length)
    factor = 1.0 / (48.0 * math.sqrt(CHANNELS))
    return (np.sinc(centred) * window * factor).reshape(TAPS, CHANNELS).astype(np.float32)


def tap_blocks():
    return filter_table().reshape(TAPS, SLOW, FAST).transpose(1, 0, 2)


def turn_blocks():
    angle = np.arange(SLOW)[:, None] * np.arange(CHANNELS)[None, :] % CHANNELS
    angle = angle * (2.0 * math.pi / CHANNELS)
    both = np.concatenate([np.cos(angle), np.sin(angle)]).astype(np.float32)
    return both.reshape(2 * SLOW, SLOW, FAST).transpose(1, 0, 2)


def last_table():
    angle = np.arange(FAST)[:, None] * np.arange(FAST)[None, :] % FAST * (2.0 * math.pi / FAST)
    cosine, sine = np.cos(angle), np.sin(angle)
    upper = np.concatenate([cosine, sine], axis=1)
    lower = np.concatenate([-sine, cosine], axis=1)
    return np.concatenate([upper, lower], axis=0).astype(np.float32)


def fft(xs):
    n = len(xs)
    if n == 1:
        return xs
    even, odd = fft(xs[0::2]), fft(xs[1::2])
    low, high = [], []
    for k in range(n // 2):
        re, im = odd[k]
        if k == 0:
            tr, ti = re, im
        elif 4 * k == n:
            tr, ti = im, -re
        elif 8 * k == n:
            s = math.sqrt(0.5)
            tr, ti = (re + im) * s, (im - re) * s
        elif 8 * k == 3 * n:
            s = math.sqrt(0.5)
            tr, ti = (im - re) * s, (im + re) * (-s)
        else:
            c, s = math.cos(2 * math.pi * k / n), math.sin(2 * math.pi * k / n)
            tr, ti = re * c + im * s, im * c - re * s
        er, ei = even[k]
        low.append((er + tr, ei + ti))
        high.append((er - tr, ei - ti))
    return low + high


def split_inputs(r, voltages, spread, pieces):
    @pl.loop(0, SLOW)
    def _(b):
        lanes = pl.ds(pl.multiple_of(b * FAST, FAST), FAST)
        slot = b % 2
        for f in range(BLOCK):
            there = pl.ds(pl.multiple_of(f * CHANNELS + b * FAST, FAST), FAST)
            spread[slot, pl.ds(f, 8, stride=BLOCK), :] = voltages[r, :, there].astype(jnp.float32)
        for i in range(8):
            rows = spread[slot, BLOCK * i : BLOCK * i + BLOCK, :]
            pieces[i // 2, i % 2, r, :, lanes] = rows.astype(jnp.bfloat16)


def delayed_tables(i, delay, tap_ref, turn_all, last_all, taps_ref, turn_ref, last_ref):
    high, low = delay >> 7, delay & 127
    lane = lax.broadcasted_iota(jnp.int32, (1, FAST), 1)
    same = lane < FAST - low
    shift = (FAST - low) & 127

    def ahead(table, b):
        first = pltpu.roll(table[(b + high) & 31], shift, 1)
        second = pltpu.roll(table[(b + high + 1) & 31], shift, 1)
        return jnp.where(same, first, second)

    @pl.loop(0, SLOW)
    def _(b):
        rolled = ahead(tap_ref, b)
        carry = lane + b * FAST + delay >= CHANNELS
        taps_ref[i, b, 0:TAPS, :] = jnp.where(carry, 0.0, rolled)
        taps_ref[i, b, TAPS : TAPS + 8, :] = jnp.zeros((8, FAST), jnp.float32)
        taps_ref[i, b, 1 : TAPS + 1, :] += jnp.where(carry, rolled, 0.0)

    turn_ref[i] = ahead(turn_all, 0)

    @pl.loop(0, 8)
    def _(g):
        rows = pl.ds(pl.multiple_of(g * 32, 32), 32)
        for part in range(2):
            lanes = slice(part * FAST, part * FAST + FAST)
            last_ref[i, rows, lanes] = pltpu.roll(last_all[rows, lanes], shift, 1).astype(jnp.bfloat16)


def filter_frames(i, own, halo, taps_ref, xs, branch, first):
    octets = range(2) if first else range(2, 8)
    base = BLOCK if first else 0

    @pl.loop(0, SLOW)
    def _(b):
        lanes = pl.ds(pl.multiple_of(b * FAST, FAST), FAST)
        taps = [jnp.broadcast_to(taps_ref[i, b, k : k + 1, :], (8, FAST)) for k in range(TAPS + 1)]
        for r in range(2):
            if first:
                xs[r, 0:BLOCK, :] = halo[i, r, :, lanes].astype(jnp.float32)
                xs[r, BLOCK : 2 * BLOCK, :] = own[0, i, r, :, lanes].astype(jnp.float32)
            else:
                for g in range(GROUP):
                    xs[r, BLOCK * g : BLOCK * g + BLOCK, :] = own[g, i, r, :, lanes].astype(
                        jnp.float32
                    )
        for r in range(2):
            total = {}
            for s in range(8 * octets[0] - TAPS, 8 * octets[-1] + 1):
                window = xs[r, base + s : base + s + 8, :]
                for o in octets:
                    k = 8 * o - s
                    if 0 <= k <= TAPS:
                        term = taps[k] * window
                        total[o] = total[o] + term if o in total else term
                    if k == 0:
                        branch[r, b, 8 * o : 8 * o + 8, :] = total[o]


def slow_transform(i, turn_ref, branch, inner, first):
    @pl.loop(*((0, 2) if first else (2, 8)))
    def _(o):
        rows = pl.ds(pl.multiple_of(o * 8, 8), 8)
        points = [(branch[0, b, rows, :], branch[1, b, rows, :]) for b in range(SLOW)]
        for k, (re, im) in enumerate(fft(points)):
            c = jnp.broadcast_to(turn_ref[i, k : k + 1, :], (8, FAST))
            s = jnp.broadcast_to(turn_ref[i, SLOW + k : SLOW + k + 1, :], (8, FAST))
            inner[k, rows, 0:FAST] = re * c + im * s
            inner[k, rows, FAST : 2 * FAST] = im * c - re * s


def fast_transform(i, last_ref, inner, flat):
    @pl.loop(0, 8)
    def _(g):
        points = inner[pl.ds(g * 4, 4), :, :].reshape(4 * 64, 2 * FAST).astype(jnp.bfloat16)
        result = lax.dot_general(
            last_ref[i], points, (((1,), (1,)), ((), ())), preferred_element_type=jnp.float32
        )
        for r in range(2):
            for t in range(2):
                for l in range(16):
                    piece = result[r * FAST + 8 * l : r * FAST + 8 * l + 8, t * FAST : t * FAST + FAST]
                    flat[r, pl.ds(l * 128 + g * 2 + t, 8, stride=16), :] = piece


def widen(block, got, wide):
    @pl.loop(0, 2)
    def _(stn):
        for ct in range(4):
            for y in range(4):
                for i in range(2):
                    for r in range(2):
                        row = stn * 32 + (ct * 4 + y) * 2 + i
                        place = pl.ds(pl.multiple_of(row * 16, 16), 16)
                        wide[r, place, :] = got[stn, block * 16 + y * 4 + ct, i, r, :, :].astype(
                            jnp.float32
                        )


def reorder(j, lanes, wide, packed):
    for r in range(2):
        for g in range(4):
            rows = [wide[r, pl.ds((g * 16 + h * 8) * 16 + j, 8, stride=16), :] for h in range(2)]
            place = slice(r * 64 + g * 16, r * 64 + g * 16 + 16)
            packed[j, place, lanes] = jnp.concatenate(rows, axis=0).astype(jnp.bfloat16)


def reorder_all(step, wide, packed):
    lanes = pl.ds(pl.multiple_of(step * FAST, FAST), FAST)

    @pl.loop(0, 16, step=4)
    def _(j0):
        for u in range(4):
            reorder(j0 + u, lanes, wide, packed)


def products(j, mine, begin, end, packed):
    lanes = slice(begin * FAST, end * FAST)
    shape = (64, (end - begin) * FAST)
    even = (lax.broadcasted_iota(jnp.int32, shape, 1) % FAST < 64).astype(jnp.float32)
    even = even.astype(jnp.bfloat16)
    left = jnp.concatenate(
        [packed[j, pl.ds(pl.multiple_of(r * 64 + mine * 32, 32), 32), lanes] for r in range(2)], axis=0
    )
    left = jnp.concatenate([left * even, left * (1 - even)], axis=0)
    return lax.dot_general(
        left, packed[j, :, lanes], (((1,), (1,)), ((), ())), preferred_element_type=jnp.float32
    )


def first_six(mine, packed, sums):
    @pl.loop(0, 16, step=2)
    def _(j0):
        for u in range(2):
            sums[j0 + u] = products(j0 + u, mine, 0, 6, packed)


def last_two(mine, wide, packed, sums, out_ref):
    @pl.loop(0, 16, step=4)
    def _(j0):
        for u in range(4):
            reorder(j0 + u, slice(7 * FAST, 8 * FAST), wide, packed)
        for u in range(4):
            j = j0 + u
            both = sums[j] + products(j, mine, 6, 8, packed)
            for odd in range(2):
                grid = both[64 * odd : 64 * odd + 64]
                k = 2 * j + odd
                out_ref[0, k, :, :] = (grid[0:32, 0:64] + grid[32:64, 64:128]) * (1.0 / FRAMES)
                out_ref[1, k, :, :] = (grid[32:64, 0:64] - grid[0:32, 64:128]) * (1.0 / FRAMES)


def whole_kernel(
    delays,
    voltages_hbm,
    tap_hbm,
    turn_hbm,
    last_hbm,
    out_ref,
    voltages,
    tap_all,
    turn_all,
    last_all,
    taps_ref,
    turn_ref,
    last_ref,
    spread,
    pieces,
    own,
    halo,
    chunks,
    got,
    xs,
    branch,
    inner,
    flat,
    wide,
    packed,
    sums,
    load_sem,
    all_sem,
    near_send,
    near_recv,
    halo_send,
    halo_recv,
    far_send,
    far_recv,
    twin_send,
    twin_recv,
):
    tm, ct, stn = lax.axis_index("tm"), lax.axis_index("ct"), lax.axis_index("stn")
    me = tm * 4 + ct
    y, block, column = tm % 4, tm // 4, tm // 8

    loads = [
        pltpu.make_async_copy(voltages_hbm.at[0], voltages.at[0], load_sem.at[0]),
        pltpu.make_async_copy(voltages_hbm.at[1], voltages.at[1], load_sem.at[1]),
        pltpu.make_async_copy(tap_hbm, tap_all, load_sem.at[2]),
        pltpu.make_async_copy(turn_hbm, turn_all, load_sem.at[3]),
        pltpu.make_async_copy(last_hbm, last_all, load_sem.at[4]),
    ]
    for load in loads:
        load.start()

    def along_y(offset):
        return {"tm": block * 4 + (y + offset) % 4, "ct": ct}

    def along_z(offset):
        z = ((block % 2) * 4 + ct + offset) % 8
        return {"tm": column * 8 + (z // 4) * 4 + y, "ct": z % 4}

    def along_x(offset):
        return {"tm": (tm + 8 * offset) % 32, "ct": ct}

    diagonal = {"tm": (tm + jnp.where(block % 2 == 0, 28, 4)) % 32, "ct": ct}
    greeted = [along_y(o) for o in range(1, 4)] + [{"stn": 1 - stn}, diagonal]
    greeted += [along_z(o) for o in range(1, 8)] + [along_x(o) for o in range(1, 4)]
    barrier = pltpu.get_barrier_semaphore()
    for other in greeted:
        pl.semaphore_signal(barrier, inc=1, device_id=other, device_id_type=MESH)

    @pl.when(block == 0)
    def _():
        halo[...] = jnp.zeros_like(halo)

    loads[0].wait()
    split_inputs(0, voltages, spread, pieces)
    pl.semaphore_wait(barrier, len(greeted))

    def near(i, r, offset):
        other = (y + offset) % GROUP
        return pltpu.make_async_remote_copy(
            src_ref=pieces.at[other, i, r],
            dst_ref=own.at[y, i, r],
            send_sem=near_send.at[i, r, offset],
            recv_sem=near_recv.at[i, r, y],
            device_id={"tm": block * 4 + other},
            device_id_type=MESH,
        )

    def near_arrival(i, r, source):
        return pltpu.make_async_copy(
            pieces.at[0, i, r], own.at[source, i, r], near_recv.at[i, r, source]
        )

    def halo_copy(i, r):
        return pltpu.make_async_remote_copy(
            src_ref=own.at[GROUP - 1, i, r],
            dst_ref=halo.at[i, r],
            send_sem=halo_send.at[i, r],
            recv_sem=halo_recv.at[i, r],
            device_id={"tm": (tm + GROUP) % 32},
            device_id_type=MESH,
        )

    def pass_on(i):
        for r in range(2):
            near_arrival(i, r, GROUP - 1).wait()

            @pl.when(block < 7)
            def _():
                halo_copy(i, r).start()

    def exchange(i, r):
        pltpu.make_async_copy(pieces.at[y, i, r], own.at[y, i, r], near_recv.at[i, r, y]).start()
        for offset in (1, 3, 2):
            near(i, r, offset).start()

    exchange(0, 0)
    loads[1].wait()
    split_inputs(1, voltages, spread, pieces)
    exchange(0, 1)

    @pl.when(y == GROUP - 1)
    def _():
        exchange(1, 0)
        exchange(1, 1)


    for offset in range(1, 8):
        pl.semaphore_signal(all_sem.at[0], inc=1, device_id=along_z(offset), device_id_type=MESH)
    pl.semaphore_wait(all_sem.at[0], 7)
    for offset in range(1, 4):
        pl.semaphore_signal(all_sem.at[1], inc=1, device_id=along_y(offset), device_id_type=MESH)

    for load in loads[2:]:
        load.wait()
    for i in range(2):
        delayed_tables(
            i, delays[2 * y + i], tap_all, turn_all, last_all, taps_ref, turn_ref, last_ref
        )
        if i == 0:
            pass_on(0)

    def far(l, i):
        return pltpu.make_async_remote_copy(
            src_ref=chunks.at[l, i],
            dst_ref=got.at[stn, me, i],
            send_sem=far_send,
            recv_sem=far_recv.at[block],
            device_id={"tm": l // 4, "ct": l % 4},
            device_id_type=MESH,
        )

    @pl.loop(0, 2)
    def _(i):
        for r in range(2):
            for source in range(GROUP - 1):
                near_arrival(i, r, source).wait()

            @pl.when((i == 0) & (y < GROUP - 1))
            def _():
                exchange(1, r)

        filter_frames(i, own, halo, taps_ref, xs, branch, False)
        slow_transform(i, turn_ref, branch, inner, False)

        @pl.when(i == 0)
        def _():
            pass_on(1)

        @pl.when(block > 0)
        def _():
            for r in range(2):
                halo_copy(i, r).wait_recv()

        filter_frames(i, own, halo, taps_ref, xs, branch, True)
        slow_transform(i, turn_ref, branch, inner, True)
        fast_transform(i, last_ref, inner, flat)

        @pl.when(i == 0)
        def _():
            pl.semaphore_wait(all_sem.at[1], 3)

        @pl.loop(0, OWNERS, step=4)
        def _(j0):
            for u in range(4):
                l = (me + j0 + u) % OWNERS
                rows = pl.ds(pl.multiple_of(l * 16, 16), 16)
                for r in range(2):
                    chunks[l, i, r, :, :] = flat[r, rows, :].astype(jnp.bfloat16)

            @pl.when(j0 == 0)
            def _():
                pltpu.make_async_copy(
                    chunks.at[me, i], got.at[stn, me, i], far_recv.at[block]
                ).start()

            @pl.when(j0 > 0)
            def _():
                far((me + j0) % OWNERS, i).start()

            for u in range(1, 4):
                far((me + j0 + u) % OWNERS, i).start()

    def twin(p):
        rows = got.at[stn, pl.ds(p * 16, 16)]
        return pltpu.make_async_remote_copy(
            src_ref=rows,
            dst_ref=rows,
            send_sem=twin_send.at[p],
            recv_sem=twin_recv.at[p],
            device_id={"stn": 1 - stn},
            device_id_type=MESH,
        )

    def turn(step):
        return (block + 7 - step) % 8

    def hand_over(step):
        rows = got.at[stn, pl.ds(turn(step) * 16, 16)]
        pltpu.make_async_copy(rows, rows, far_recv.at[turn(step)]).wait()
        twin(turn(step)).start()

    def take(step):
        twin(turn(step)).wait_recv()
        widen(turn(step), got, wide)

    hand_over(0)

    @pl.loop(0, 6)
    def _(step):
        @pl.when(step < 5)
        def _():
            hand_over(step + 1)

        take(step)
        reorder_all(step, wide, packed)

    first_six(stn, packed, sums)
    hand_over(6)
    hand_over(7)
    take(6)
    reorder_all(6, wide, packed)
    take(7)
    last_two(stn, wide, packed, sums, out_ref)

    for i in range(2):
        for r in range(2):
            for offset in (1, 3, 2):
                near(i, r, offset).wait_send()

            @pl.when(block < 7)
            def _():
                halo_copy(i, r).wait_send()

    for p in range(8):
        twin(p).wait_send()
    sent = chunks.at[pl.ds(0, OWNERS - 1)]
    pltpu.make_async_copy(sent, sent, far_send).wait()


def on_device(voltages, delays):
    dma = pltpu.SemaphoreType.DMA
    f32, bf16 = jnp.float32, jnp.bfloat16
    return pl.pallas_call(
        whole_kernel,
        out_shape=jax.ShapeDtypeStruct((2, SLOW, 32, 64), f32),
        in_specs=[pl.BlockSpec(memory_space=pltpu.SMEM)] + [pl.BlockSpec(memory_space=pl.ANY)] * 4,
        out_specs=pl.BlockSpec(memory_space=pltpu.VMEM),
        scratch_shapes=[
            pltpu.VMEM((2, 8, BLOCK * CHANNELS), bf16),
            pltpu.VMEM((SLOW, TAPS, FAST), f32),
            pltpu.VMEM((SLOW, 2 * SLOW, FAST), f32),
            pltpu.VMEM((2 * FAST, 2 * FAST), f32),
            pltpu.VMEM((2, SLOW, 24, FAST), f32),
            pltpu.VMEM((2, 2 * SLOW, FAST), f32),
            pltpu.VMEM((2, 2 * FAST, 2 * FAST), bf16),
            pltpu.VMEM((2, 8 * BLOCK, FAST), f32),
            pltpu.VMEM((GROUP, 2, 2, BLOCK, CHANNELS), bf16),
            pltpu.VMEM((GROUP, 2, 2, BLOCK, CHANNELS), bf16),
            pltpu.VMEM((2, 2, BLOCK, CHANNELS), bf16),
            pltpu.VMEM((OWNERS, 2, 2, 16, FAST), bf16),
            pltpu.VMEM((2, OWNERS, 2, 2, 16, FAST), bf16),
            pltpu.VMEM((2, 64, FAST), f32),
            pltpu.VMEM((2, SLOW, 64, FAST), f32),
            pltpu.VMEM((SLOW, 64, 2 * FAST), f32),
            pltpu.VMEM((2, FAST * 16, FAST), f32),
            pltpu.VMEM((2, 64 * 16, FAST), f32),
            pltpu.VMEM((16, FAST, 8 * FAST), bf16),
            pltpu.VMEM((16, FAST, FAST), f32),
            dma((5,)),
            pltpu.SemaphoreType.REGULAR((2,)),
            dma((2, 2, GROUP)),
            dma((2, 2, GROUP)),
            dma((2, 2)),
            dma((2, 2)),
            dma,
            dma((8,)),
            dma((8,)),
            dma((8,)),
        ],
        compiler_params=pltpu.CompilerParams(
            collective_id=0, has_side_effects=True, vmem_limit_bytes=56 << 20
        ),
    )(delays, voltages, tap_blocks(), turn_blocks(), last_table())


def solution(mesh):
    return jax.shard_map(
        on_device,
        mesh=mesh,
        in_specs=(P(None, ("stn", "ct"), "tm"), P(("stn", "ct"))),
        out_specs=P(None, ("tm", "ct"), "stn", None),
        check_vma=False,
    )
```

```python
import math

import jax
import jax.numpy as jnp
import numpy as np
from jax import lax
from jax.experimental import pallas as pl
from jax.experimental.pallas import tpu as pltpu
from jax.sharding import PartitionSpec as P

CHANNELS = 4096
TAPS = 16
SLOW = 32
FAST = 128
BLOCK = 16
GROUP = 4
FRAMES = 512
OWNERS = 128
MESH = pl.DeviceIdType.MESH


def filter_table():
    length = TAPS * CHANNELS
    index = np.arange(length, dtype=np.float64)
    centred = (index - length / 2) / CHANNELS
    window = 0.5 - 0.5 * np.cos(2.0 * math.pi * index / length)
    factor = 1.0 / (48.0 * math.sqrt(CHANNELS))
    return (np.sinc(centred) * window * factor).reshape(TAPS, CHANNELS).astype(np.float32)


def tap_blocks():
    return filter_table().reshape(TAPS, SLOW, FAST).transpose(1, 0, 2)


def turn_blocks():
    angle = np.arange(SLOW)[:, None] * np.arange(CHANNELS)[None, :] % CHANNELS
    angle = angle * (2.0 * math.pi / CHANNELS)
    both = np.concatenate([np.cos(angle), np.sin(angle)]).astype(np.float32)
    return both.reshape(2 * SLOW, SLOW, FAST).transpose(1, 0, 2)


def last_table():
    angle = np.arange(FAST)[:, None] * np.arange(FAST)[None, :] % FAST * (2.0 * math.pi / FAST)
    cosine, sine = np.cos(angle), np.sin(angle)
    upper = np.concatenate([cosine, sine], axis=1)
    lower = np.concatenate([-sine, cosine], axis=1)
    return np.concatenate([upper, lower], axis=0).astype(np.float32)


def fft(xs):
    n = len(xs)
    if n == 1:
        return xs
    even, odd = fft(xs[0::2]), fft(xs[1::2])
    low, high = [], []
    for k in range(n // 2):
        re, im = odd[k]
        if k == 0:
            tr, ti = re, im
        elif 4 * k == n:
            tr, ti = im, -re
        elif 8 * k == n:
            s = math.sqrt(0.5)
            tr, ti = (re + im) * s, (im - re) * s
        elif 8 * k == 3 * n:
            s = math.sqrt(0.5)
            tr, ti = (im - re) * s, (im + re) * (-s)
        else:
            c, s = math.cos(2 * math.pi * k / n), math.sin(2 * math.pi * k / n)
            tr, ti = re * c + im * s, im * c - re * s
        er, ei = even[k]
        low.append((er + tr, ei + ti))
        high.append((er - tr, ei - ti))
    return low + high


def split_inputs(r, voltages, spread, pieces):
    @pl.loop(0, SLOW)
    def _(b):
        lanes = pl.ds(pl.multiple_of(b * FAST, FAST), FAST)
        slot = b % 2
        for f in range(BLOCK):
            there = pl.ds(pl.multiple_of(f * CHANNELS + b * FAST, FAST), FAST)
            spread[slot, pl.ds(f, 8, stride=BLOCK), :] = voltages[r, :, there].astype(jnp.float32)
        for i in range(8):
            rows = spread[slot, BLOCK * i : BLOCK * i + BLOCK, :]
            pieces[i // 2, i % 2, r, :, lanes] = rows.astype(jnp.bfloat16)


def delayed_tables(i, delay, tap_ref, turn_all, last_all, taps_ref, turn_ref, last_ref):
    high, low = delay >> 7, delay & 127
    lane = lax.broadcasted_iota(jnp.int32, (1, FAST), 1)
    same = lane < FAST - low
    shift = (FAST - low) & 127

    def ahead(table, b):
        first = pltpu.roll(table[(b + high) & 31], shift, 1)
        second = pltpu.roll(table[(b + high + 1) & 31], shift, 1)
        return jnp.where(same, first, second)

    @pl.loop(0, SLOW)
    def _(b):
        rolled = ahead(tap_ref, b)
        carry = lane + b * FAST + delay >= CHANNELS
        taps_ref[i, b, 0:TAPS, :] = jnp.where(carry, 0.0, rolled)
        taps_ref[i, b, TAPS : TAPS + 8, :] = jnp.zeros((8, FAST), jnp.float32)
        taps_ref[i, b, 1 : TAPS + 1, :] += jnp.where(carry, rolled, 0.0)

    turn_ref[i] = ahead(turn_all, 0)

    @pl.loop(0, 8)
    def _(g):
        rows = pl.ds(pl.multiple_of(g * 32, 32), 32)
        for part in range(2):
            lanes = slice(part * FAST, part * FAST + FAST)
            last_ref[i, rows, lanes] = pltpu.roll(last_all[rows, lanes], shift, 1).astype(jnp.bfloat16)


def filter_frames(i, own, halo, taps_ref, xs, branch, first):
    octets = range(2) if first else range(2, 8)
    base = BLOCK if first else 0

    @pl.loop(0, SLOW)
    def _(b):
        lanes = pl.ds(pl.multiple_of(b * FAST, FAST), FAST)
        taps = [jnp.broadcast_to(taps_ref[i, b, k : k + 1, :], (8, FAST)) for k in range(TAPS + 1)]
        for r in range(2):
            if first:
                xs[r, 0:BLOCK, :] = halo[i, r, :, lanes].astype(jnp.float32)
                xs[r, BLOCK : 2 * BLOCK, :] = own[0, i, r, :, lanes].astype(jnp.float32)
            else:
                for g in range(GROUP):
                    xs[r, BLOCK * g : BLOCK * g + BLOCK, :] = own[g, i, r, :, lanes].astype(
                        jnp.float32
                    )
        for r in range(2):
            total = {}
            for s in range(8 * octets[0] - TAPS, 8 * octets[-1] + 1):
                window = xs[r, base + s : base + s + 8, :]
                for o in octets:
                    k = 8 * o - s
                    if 0 <= k <= TAPS:
                        term = taps[k] * window
                        total[o] = total[o] + term if o in total else term
                    if k == 0:
                        branch[r, b, 8 * o : 8 * o + 8, :] = total[o]


def slow_transform(i, turn_ref, branch, inner, first):
    @pl.loop(*((0, 2) if first else (2, 8)))
    def _(o):
        rows = pl.ds(pl.multiple_of(o * 8, 8), 8)
        points = [(branch[0, b, rows, :], branch[1, b, rows, :]) for b in range(SLOW)]
        for k, (re, im) in enumerate(fft(points)):
            c = jnp.broadcast_to(turn_ref[i, k : k + 1, :], (8, FAST))
            s = jnp.broadcast_to(turn_ref[i, SLOW + k : SLOW + k + 1, :], (8, FAST))
            inner[k, rows, 0:FAST] = re * c + im * s
            inner[k, rows, FAST : 2 * FAST] = im * c - re * s


def fast_transform(i, last_ref, inner, flat):
    @pl.loop(0, 8)
    def _(g):
        points = inner[pl.ds(g * 4, 4), :, :].reshape(4 * 64, 2 * FAST).astype(jnp.bfloat16)
        result = lax.dot_general(
            last_ref[i], points, (((1,), (1,)), ((), ())), preferred_element_type=jnp.float32
        )
        for r in range(2):
            for t in range(2):
                for l in range(16):
                    piece = result[r * FAST + 8 * l : r * FAST + 8 * l + 8, t * FAST : t * FAST + FAST]
                    flat[r, pl.ds(l * 128 + g * 2 + t, 8, stride=16), :] = piece


def widen(block, got, wide):
    @pl.loop(0, 2)
    def _(stn):
        for ct in range(4):
            for y in range(4):
                for i in range(2):
                    for r in range(2):
                        row = stn * 32 + (ct * 4 + y) * 2 + i
                        place = pl.ds(pl.multiple_of(row * 16, 16), 16)
                        wide[r, place, :] = got[stn, block * 16 + y * 4 + ct, i, r, :, :].astype(
                            jnp.float32
                        )


def reorder(j, lanes, wide, packed):
    for r in range(2):
        for g in range(4):
            rows = [wide[r, pl.ds((g * 16 + h * 8) * 16 + j, 8, stride=16), :] for h in range(2)]
            place = slice(r * 64 + g * 16, r * 64 + g * 16 + 16)
            packed[j, place, lanes] = jnp.concatenate(rows, axis=0).astype(jnp.bfloat16)


def reorder_all(step, wide, packed):
    lanes = pl.ds(pl.multiple_of(step * FAST, FAST), FAST)

    @pl.loop(0, 16, step=4)
    def _(j0):
        for u in range(4):
            reorder(j0 + u, lanes, wide, packed)


def products(j, mine, begin, end, packed):
    lanes = slice(begin * FAST, end * FAST)
    shape = (64, (end - begin) * FAST)
    even = (lax.broadcasted_iota(jnp.int32, shape, 1) % FAST < 64).astype(jnp.float32)
    even = even.astype(jnp.bfloat16)
    left = jnp.concatenate(
        [packed[j, pl.ds(pl.multiple_of(r * 64 + mine * 32, 32), 32), lanes] for r in range(2)], axis=0
    )
    left = jnp.concatenate([left * even, left * (1 - even)], axis=0)
    return lax.dot_general(
        left, packed[j, :, lanes], (((1,), (1,)), ((), ())), preferred_element_type=jnp.float32
    )


def first_six(mine, packed, sums):
    @pl.loop(0, 16, step=2)
    def _(j0):
        for u in range(2):
            sums[j0 + u] = products(j0 + u, mine, 0, 6, packed)


def last_two(mine, wide, packed, sums, out_ref):
    @pl.loop(0, 16, step=4)
    def _(j0):
        for u in range(4):
            reorder(j0 + u, slice(7 * FAST, 8 * FAST), wide, packed)
        for u in range(4):
            j = j0 + u
            both = sums[j] + products(j, mine, 6, 8, packed)
            for odd in range(2):
                grid = both[64 * odd : 64 * odd + 64]
                k = 2 * j + odd
                out_ref[0, k, :, :] = (grid[0:32, 0:64] + grid[32:64, 64:128]) * (1.0 / FRAMES)
                out_ref[1, k, :, :] = (grid[32:64, 0:64] - grid[0:32, 64:128]) * (1.0 / FRAMES)


def whole_kernel(
    delays,
    voltages_hbm,
    tap_hbm,
    turn_hbm,
    last_hbm,
    out_ref,
    voltages,
    tap_all,
    turn_all,
    last_all,
    taps_ref,
    turn_ref,
    last_ref,
    spread,
    pieces,
    own,
    halo,
    chunks,
    got,
    xs,
    branch,
    inner,
    flat,
    wide,
    packed,
    sums,
    load_sem,
    all_sem,
    near_send,
    near_recv,
    halo_send,
    halo_recv,
    far_send,
    far_recv,
    twin_send,
    twin_recv,
):
    tm, ct, stn = lax.axis_index("tm"), lax.axis_index("ct"), lax.axis_index("stn")
    me = tm * 4 + ct
    y, block, column = tm % 4, tm // 4, tm // 8

    loads = [
        pltpu.make_async_copy(voltages_hbm.at[0], voltages.at[0], load_sem.at[0]),
        pltpu.make_async_copy(voltages_hbm.at[1], voltages.at[1], load_sem.at[1]),
        pltpu.make_async_copy(tap_hbm, tap_all, load_sem.at[2]),
        pltpu.make_async_copy(turn_hbm, turn_all, load_sem.at[3]),
        pltpu.make_async_copy(last_hbm, last_all, load_sem.at[4]),
    ]
    for load in loads:
        load.start()

    def along_y(offset):
        return {"tm": block * 4 + (y + offset) % 4, "ct": ct}

    def along_z(offset):
        z = ((block % 2) * 4 + ct + offset) % 8
        return {"tm": column * 8 + (z // 4) * 4 + y, "ct": z % 4}

    def along_x(offset):
        return {"tm": (tm + 8 * offset) % 32, "ct": ct}

    diagonal = {"tm": (tm + jnp.where(block % 2 == 0, 28, 4)) % 32, "ct": ct}
    greeted = [along_y(o) for o in range(1, 4)] + [{"stn": 1 - stn}, diagonal]
    greeted += [along_z(o) for o in range(1, 8)] + [along_x(o) for o in range(1, 4)]
    barrier = pltpu.get_barrier_semaphore()
    for other in greeted:
        pl.semaphore_signal(barrier, inc=1, device_id=other, device_id_type=MESH)

    @pl.when(block == 0)
    def _():
        halo[...] = jnp.zeros_like(halo)

    loads[0].wait()
    split_inputs(0, voltages, spread, pieces)
    pl.semaphore_wait(barrier, len(greeted))

    def near(i, r, offset):
        other = (y + offset) % GROUP
        return pltpu.make_async_remote_copy(
            src_ref=pieces.at[other, i, r],
            dst_ref=own.at[y, i, r],
            send_sem=near_send.at[i, r, offset],
            recv_sem=near_recv.at[i, r, y],
            device_id={"tm": block * 4 + other},
            device_id_type=MESH,
        )

    def near_arrival(i, r, source):
        return pltpu.make_async_copy(
            pieces.at[0, i, r], own.at[source, i, r], near_recv.at[i, r, source]
        )

    def halo_copy(i, r):
        return pltpu.make_async_remote_copy(
            src_ref=own.at[GROUP - 1, i, r],
            dst_ref=halo.at[i, r],
            send_sem=halo_send.at[i, r],
            recv_sem=halo_recv.at[i, r],
            device_id={"tm": (tm + GROUP) % 32},
            device_id_type=MESH,
        )

    def pass_on(i):
        for r in range(2):
            near_arrival(i, r, GROUP - 1).wait()

            @pl.when(block < 7)
            def _():
                halo_copy(i, r).start()

    def exchange(i, r):
        pltpu.make_async_copy(pieces.at[y, i, r], own.at[y, i, r], near_recv.at[i, r, y]).start()
        for offset in (1, 3, 2):
            near(i, r, offset).start()

    exchange(0, 0)
    loads[1].wait()
    split_inputs(1, voltages, spread, pieces)
    exchange(0, 1)

    @pl.when(y == GROUP - 1)
    def _():
        exchange(1, 0)
        exchange(1, 1)


    for offset in range(1, 8):
        pl.semaphore_signal(all_sem.at[0], inc=1, device_id=along_z(offset), device_id_type=MESH)
    pl.semaphore_wait(all_sem.at[0], 7)
    for offset in range(1, 4):
        pl.semaphore_signal(all_sem.at[1], inc=1, device_id=along_y(offset), device_id_type=MESH)

    for load in loads[2:]:
        load.wait()
    for i in range(2):
        delayed_tables(
            i, delays[2 * y + i], tap_all, turn_all, last_all, taps_ref, turn_ref, last_ref
        )
        if i == 0:
            pass_on(0)

    def far(l, i):
        return pltpu.make_async_remote_copy(
            src_ref=chunks.at[l, i],
            dst_ref=got.at[stn, me, i],
            send_sem=far_send,
            recv_sem=far_recv.at[block],
            device_id={"tm": l // 4, "ct": l % 4},
            device_id_type=MESH,
        )

    @pl.loop(0, 2)
    def _(i):
        for r in range(2):
            for source in range(GROUP - 1):
                near_arrival(i, r, source).wait()

            @pl.when((i == 0) & (y < GROUP - 1))
            def _():
                exchange(1, r)

        filter_frames(i, own, halo, taps_ref, xs, branch, False)
        slow_transform(i, turn_ref, branch, inner, False)

        @pl.when(i == 0)
        def _():
            pass_on(1)

        @pl.when(block > 0)
        def _():
            for r in range(2):
                halo_copy(i, r).wait_recv()

        filter_frames(i, own, halo, taps_ref, xs, branch, True)
        slow_transform(i, turn_ref, branch, inner, True)
        fast_transform(i, last_ref, inner, flat)

        @pl.when(i == 0)
        def _():
            pl.semaphore_wait(all_sem.at[1], 3)

        @pl.loop(0, OWNERS, step=4)
        def _(j0):
            for u in range(4):
                l = (me + j0 + u) % OWNERS
                rows = pl.ds(pl.multiple_of(l * 16, 16), 16)
                for r in range(2):
                    chunks[l, i, r, :, :] = flat[r, rows, :].astype(jnp.bfloat16)

            @pl.when(j0 == 0)
            def _():
                pltpu.make_async_copy(
                    chunks.at[me, i], got.at[stn, me, i], far_recv.at[block]
                ).start()

            @pl.when(j0 > 0)
            def _():
                far((me + j0) % OWNERS, i).start()

            for u in range(1, 4):
                far((me + j0 + u) % OWNERS, i).start()

    def twin(p):
        rows = got.at[stn, pl.ds(p * 16, 16)]
        return pltpu.make_async_remote_copy(
            src_ref=rows,
            dst_ref=rows,
            send_sem=twin_send.at[p],
            recv_sem=twin_recv.at[p],
            device_id={"stn": 1 - stn},
            device_id_type=MESH,
        )

    def turn(step):
        return (block + 7 - step) % 8

    def hand_over(step):
        rows = got.at[stn, pl.ds(turn(step) * 16, 16)]
        pltpu.make_async_copy(rows, rows, far_recv.at[turn(step)]).wait()
        twin(turn(step)).start()

    def take(step):
        twin(turn(step)).wait_recv()
        widen(turn(step), got, wide)

    hand_over(0)

    @pl.loop(0, 6)
    def _(step):
        @pl.when(step < 5)
        def _():
            hand_over(step + 1)

        take(step)
        reorder_all(step, wide, packed)

    first_six(stn, packed, sums)
    hand_over(6)
    hand_over(7)
    take(6)
    reorder_all(6, wide, packed)
    take(7)
    last_two(stn, wide, packed, sums, out_ref)

    for i in range(2):
        for r in range(2):
            for offset in (1, 3, 2):
                near(i, r, offset).wait_send()

            @pl.when(block < 7)
            def _():
                halo_copy(i, r).wait_send()

    for p in range(8):
        twin(p).wait_send()
    sent = chunks.at[pl.ds(0, OWNERS - 1)]
    pltpu.make_async_copy(sent, sent, far_send).wait()


def on_device(voltages, delays):
    dma = pltpu.SemaphoreType.DMA
    f32, bf16 = jnp.float32, jnp.bfloat16
    return pl.pallas_call(
        whole_kernel,
        out_shape=jax.ShapeDtypeStruct((2, SLOW, 32, 64), f32),
        in_specs=[pl.BlockSpec(memory_space=pltpu.SMEM)] + [pl.BlockSpec(memory_space=pl.ANY)] * 4,
        out_specs=pl.BlockSpec(memory_space=pltpu.VMEM),
        scratch_shapes=[
            pltpu.VMEM((2, 8, BLOCK * CHANNELS), bf16),
            pltpu.VMEM((SLOW, TAPS, FAST), f32),
            pltpu.VMEM((SLOW, 2 * SLOW, FAST), f32),
            pltpu.VMEM((2 * FAST, 2 * FAST), f32),
            pltpu.VMEM((2, SLOW, 24, FAST), f32),
            pltpu.VMEM((2, 2 * SLOW, FAST), f32),
            pltpu.VMEM((2, 2 * FAST, 2 * FAST), bf16),
            pltpu.VMEM((2, 8 * BLOCK + BLOCK, FAST), f32),
            pltpu.VMEM((GROUP, 2, 2, BLOCK, CHANNELS), bf16),
            pltpu.VMEM((GROUP, 2, 2, BLOCK, CHANNELS), bf16),
            pltpu.VMEM((2, 2, BLOCK, CHANNELS), bf16),
            pltpu.VMEM((OWNERS, 2, 2, 16, FAST), bf16),
            pltpu.VMEM((2, OWNERS, 2, 2, 16, FAST), bf16),
            pltpu.VMEM((2, 64, FAST), f32),
            pltpu.VMEM((2, SLOW, 64, FAST), f32),
            pltpu.VMEM((SLOW, 64, 2 * FAST), f32),
            pltpu.VMEM((2, FAST * 16 + 16, FAST), f32),
            pltpu.VMEM((2, 64 * 16 + 16, FAST), f32),
            pltpu.VMEM((16, FAST, 8 * FAST), bf16),
            pltpu.VMEM((16, FAST, FAST), f32),
            dma((5,)),
            pltpu.SemaphoreType.REGULAR((2,)),
            dma((2, 2, GROUP)),
            dma((2, 2, GROUP)),
            dma((2, 2)),
            dma((2, 2)),
            dma,
            dma((8,)),
            dma((8,)),
            dma((8,)),
        ],
        compiler_params=pltpu.CompilerParams(
            collective_id=0, has_side_effects=True, vmem_limit_bytes=56 << 20
        ),
    )(delays, voltages, tap_blocks(), turn_blocks(), last_table())


def solution(mesh):
    return jax.shard_map(
        on_device,
        mesh=mesh,
        in_specs=(P(None, ("stn", "ct"), "tm"), P(("stn", "ct"))),
        out_specs=P(None, ("tm", "ct"), "stn", None),
        check_vma=False,
    )
```

```python
import math

import jax
import jax.numpy as jnp
import numpy as np
from jax import lax
from jax.experimental import pallas as pl
from jax.experimental.pallas import tpu as pltpu
from jax.sharding import PartitionSpec as P

CHANNELS = 4096
TAPS = 16
SLOW = 32
FAST = 128
BLOCK = 16
GROUP = 4
FRAMES = 512
OWNERS = 128
MESH = pl.DeviceIdType.MESH


def filter_table():
    length = TAPS * CHANNELS
    index = np.arange(length, dtype=np.float64)
    centred = (index - length / 2) / CHANNELS
    window = 0.5 - 0.5 * np.cos(2.0 * math.pi * index / length)
    factor = 1.0 / (48.0 * math.sqrt(CHANNELS))
    return (np.sinc(centred) * window * factor).reshape(TAPS, CHANNELS).astype(np.float32)


def tap_blocks():
    return filter_table().reshape(TAPS, SLOW, FAST).transpose(1, 0, 2)


def turn_blocks():
    angle = np.arange(SLOW)[:, None] * np.arange(CHANNELS)[None, :] % CHANNELS
    angle = angle * (2.0 * math.pi / CHANNELS)
    both = np.concatenate([np.cos(angle), np.sin(angle)]).astype(np.float32)
    return both.reshape(2 * SLOW, SLOW, FAST).transpose(1, 0, 2)


def last_table():
    angle = np.arange(FAST)[:, None] * np.arange(FAST)[None, :] % FAST * (2.0 * math.pi / FAST)
    cosine, sine = np.cos(angle), np.sin(angle)
    upper = np.concatenate([cosine, sine], axis=1)
    lower = np.concatenate([-sine, cosine], axis=1)
    return np.concatenate([upper, lower], axis=0).astype(np.float32)


def fft(xs):
    n = len(xs)
    if n == 1:
        return xs
    even, odd = fft(xs[0::2]), fft(xs[1::2])
    low, high = [], []
    for k in range(n // 2):
        re, im = odd[k]
        if k == 0:
            tr, ti = re, im
        elif 4 * k == n:
            tr, ti = im, -re
        elif 8 * k == n:
            s = math.sqrt(0.5)
            tr, ti = (re + im) * s, (im - re) * s
        elif 8 * k == 3 * n:
            s = math.sqrt(0.5)
            tr, ti = (im - re) * s, (im + re) * (-s)
        else:
            c, s = math.cos(2 * math.pi * k / n), math.sin(2 * math.pi * k / n)
            tr, ti = re * c + im * s, im * c - re * s
        er, ei = even[k]
        low.append((er + tr, ei + ti))
        high.append((er - tr, ei - ti))
    return low + high


def split_inputs(r, voltages, spread, pieces):
    @pl.loop(0, SLOW)
    def _(b):
        lanes = pl.ds(pl.multiple_of(b * FAST, FAST), FAST)
        slot = b % 2
        for f in range(BLOCK):
            there = pl.ds(pl.multiple_of(f * CHANNELS + b * FAST, FAST), FAST)
            spread[slot, pl.ds(f, 8, stride=BLOCK), :] = voltages[r, :, there].astype(jnp.float32)
        for i in range(8):
            rows = spread[slot, BLOCK * i : BLOCK * i + BLOCK, :]
            pieces[i // 2, i % 2, r, :, lanes] = rows.astype(jnp.bfloat16)


def delayed_tables(i, delay, tap_ref, turn_all, last_all, taps_ref, turn_ref, last_ref):
    high, low = delay >> 7, delay & 127
    lane = lax.broadcasted_iota(jnp.int32, (1, FAST), 1)
    same = lane < FAST - low
    shift = (FAST - low) & 127

    def ahead(table, b):
        first = pltpu.roll(table[(b + high) & 31], shift, 1)
        second = pltpu.roll(table[(b + high + 1) & 31], shift, 1)
        return jnp.where(same, first, second)

    @pl.loop(0, SLOW)
    def _(b):
        rolled = ahead(tap_ref, b)
        carry = lane + b * FAST + delay >= CHANNELS
        taps_ref[i, b, 0:TAPS, :] = jnp.where(carry, 0.0, rolled)
        taps_ref[i, b, TAPS : TAPS + 8, :] = jnp.zeros((8, FAST), jnp.float32)
        taps_ref[i, b, 1 : TAPS + 1, :] += jnp.where(carry, rolled, 0.0)

    turn_ref[i] = ahead(turn_all, 0)

    @pl.loop(0, 8)
    def _(g):
        rows = pl.ds(pl.multiple_of(g * 32, 32), 32)
        for part in range(2):
            lanes = slice(part * FAST, part * FAST + FAST)
            last_ref[i, rows, lanes] = pltpu.roll(last_all[rows, lanes], shift, 1).astype(jnp.bfloat16)


def filter_frames(i, own, halo, taps_ref, xs, branch, first):
    octets = range(2) if first else range(2, 8)
    base = BLOCK if first else 0

    @pl.loop(0, SLOW)
    def _(b):
        lanes = pl.ds(pl.multiple_of(b * FAST, FAST), FAST)
        taps = [jnp.broadcast_to(taps_ref[i, b, k : k + 1, :], (8, FAST)) for k in range(TAPS + 1)]
        for r in range(2):
            if first:
                xs[r, 0:BLOCK, :] = halo[i, r, :, lanes].astype(jnp.float32)
                xs[r, BLOCK : 2 * BLOCK, :] = own[0, i, r, :, lanes].astype(jnp.float32)
            else:
                for g in range(GROUP):
                    xs[r, BLOCK * g : BLOCK * g + BLOCK, :] = own[g, i, r, :, lanes].astype(
                        jnp.float32
                    )
        for r in range(2):
            total = {}
            for s in range(8 * octets[0] - TAPS, 8 * octets[-1] + 1):
                window = xs[r, base + s : base + s + 8, :]
                for o in octets:
                    k = 8 * o - s
                    if 0 <= k <= TAPS:
                        term = taps[k] * window
                        total[o] = total[o] + term if o in total else term
                    if k == 0:
                        branch[r, b, 8 * o : 8 * o + 8, :] = total[o]


def slow_transform(i, turn_ref, branch, inner, first):
    @pl.loop(*((0, 2) if first else (2, 8)))
    def _(o):
        rows = pl.ds(pl.multiple_of(o * 8, 8), 8)
        points = [(branch[0, b, rows, :], branch[1, b, rows, :]) for b in range(SLOW)]
        for k, (re, im) in enumerate(fft(points)):
            c = jnp.broadcast_to(turn_ref[i, k : k + 1, :], (8, FAST))
            s = jnp.broadcast_to(turn_ref[i, SLOW + k : SLOW + k + 1, :], (8, FAST))
            inner[k, rows, 0:FAST] = re * c + im * s
            inner[k, rows, FAST : 2 * FAST] = im * c - re * s


def fast_transform(i, last_ref, inner, flat):
    @pl.loop(0, 8)
    def _(g):
        points = inner[pl.ds(g * 4, 4), :, :].reshape(4 * 64, 2 * FAST).astype(jnp.bfloat16)
        result = lax.dot_general(
            last_ref[i], points, (((1,), (1,)), ((), ())), preferred_element_type=jnp.float32
        )
        for r in range(2):
            for t in range(2):
                for l in range(16):
                    piece = result[r * FAST + 8 * l : r * FAST + 8 * l + 8, t * FAST : t * FAST + FAST]
                    flat[r, pl.ds(l * 128 + g * 2 + t, 8, stride=16), :] = piece


def widen(block, got, wide):
    @pl.loop(0, 2)
    def _(stn):
        for ct in range(4):
            for y in range(4):
                for i in range(2):
                    for r in range(2):
                        row = stn * 32 + (ct * 4 + y) * 2 + i
                        place = pl.ds(pl.multiple_of(row * 16, 16), 16)
                        wide[r, place, :] = got[stn, block * 16 + y * 4 + ct, i, r, :, :].astype(
                            jnp.float32
                        )


def reorder(j, lanes, wide, packed):
    for r in range(2):
        for g in range(4):
            rows = [wide[r, pl.ds((g * 16 + h * 8) * 16 + j, 8, stride=16), :] for h in range(2)]
            place = slice(r * 64 + g * 16, r * 64 + g * 16 + 16)
            packed[j, place, lanes] = jnp.concatenate(rows, axis=0).astype(jnp.bfloat16)


def reorder_all(step, wide, packed):
    lanes = pl.ds(pl.multiple_of(step * FAST, FAST), FAST)

    @pl.loop(0, 16, step=4)
    def _(j0):
        for u in range(4):
            reorder(j0 + u, lanes, wide, packed)


def products(j, mine, begin, end, packed):
    lanes = slice(begin * FAST, end * FAST)
    shape = (64, (end - begin) * FAST)
    even = (lax.broadcasted_iota(jnp.int32, shape, 1) % FAST < 64).astype(jnp.float32)
    even = even.astype(jnp.bfloat16)
    left = jnp.concatenate(
        [packed[j, pl.ds(pl.multiple_of(r * 64 + mine * 32, 32), 32), lanes] for r in range(2)], axis=0
    )
    left = jnp.concatenate([left * even, left * (1 - even)], axis=0)
    return lax.dot_general(
        left, packed[j, :, lanes], (((1,), (1,)), ((), ())), preferred_element_type=jnp.float32
    )


def first_six(mine, packed, sums):
    @pl.loop(0, 16, step=2)
    def _(j0):
        for u in range(2):
            sums[j0 + u] = products(j0 + u, mine, 0, 6, packed)


def last_two(mine, wide, packed, sums, out_ref):
    @pl.loop(0, 16, step=8)
    def _(j0):
        for u in range(8):
            reorder(j0 + u, slice(7 * FAST, 8 * FAST), wide, packed)
        for u in range(8):
            j = j0 + u
            both = sums[j] + products(j, mine, 6, 8, packed)
            for odd in range(2):
                grid = both[64 * odd : 64 * odd + 64]
                k = 2 * j + odd
                out_ref[0, k, :, :] = (grid[0:32, 0:64] + grid[32:64, 64:128]) * (1.0 / FRAMES)
                out_ref[1, k, :, :] = (grid[32:64, 0:64] - grid[0:32, 64:128]) * (1.0 / FRAMES)


def whole_kernel(
    delays,
    voltages_hbm,
    tap_hbm,
    turn_hbm,
    last_hbm,
    out_ref,
    voltages,
    tap_all,
    turn_all,
    last_all,
    taps_ref,
    turn_ref,
    last_ref,
    spread,
    pieces,
    own,
    halo,
    chunks,
    got,
    xs,
    branch,
    inner,
    flat,
    wide,
    packed,
    sums,
    load_sem,
    all_sem,
    near_send,
    near_recv,
    halo_send,
    halo_recv,
    far_send,
    far_recv,
    twin_send,
    twin_recv,
):
    tm, ct, stn = lax.axis_index("tm"), lax.axis_index("ct"), lax.axis_index("stn")
    me = tm * 4 + ct
    y, block, column = tm % 4, tm // 4, tm // 8

    loads = [
        pltpu.make_async_copy(voltages_hbm.at[0], voltages.at[0], load_sem.at[0]),
        pltpu.make_async_copy(voltages_hbm.at[1], voltages.at[1], load_sem.at[1]),
        pltpu.make_async_copy(tap_hbm, tap_all, load_sem.at[2]),
        pltpu.make_async_copy(turn_hbm, turn_all, load_sem.at[3]),
        pltpu.make_async_copy(last_hbm, last_all, load_sem.at[4]),
    ]
    for load in loads:
        load.start()

    def along_y(offset):
        return {"tm": block * 4 + (y + offset) % 4, "ct": ct}

    def along_z(offset):
        z = ((block % 2) * 4 + ct + offset) % 8
        return {"tm": column * 8 + (z // 4) * 4 + y, "ct": z % 4}

    def along_x(offset):
        return {"tm": (tm + 8 * offset) % 32, "ct": ct}

    diagonal = {"tm": (tm + jnp.where(block % 2 == 0, 28, 4)) % 32, "ct": ct}
    greeted = [along_y(o) for o in range(1, 4)] + [{"stn": 1 - stn}, diagonal]
    greeted += [along_z(o) for o in range(1, 8)] + [along_x(o) for o in range(1, 4)]
    barrier = pltpu.get_barrier_semaphore()
    for other in greeted:
        pl.semaphore_signal(barrier, inc=1, device_id=other, device_id_type=MESH)

    @pl.when(block == 0)
    def _():
        halo[...] = jnp.zeros_like(halo)

    loads[0].wait()
    split_inputs(0, voltages, spread, pieces)
    pl.semaphore_wait(barrier, len(greeted))

    def near(i, r, offset):
        other = (y + offset) % GROUP
        return pltpu.make_async_remote_copy(
            src_ref=pieces.at[other, i, r],
            dst_ref=own.at[y, i, r],
            send_sem=near_send.at[i, r, offset],
            recv_sem=near_recv.at[i, r, y],
            device_id={"tm": block * 4 + other},
            device_id_type=MESH,
        )

    def near_arrival(i, r, source):
        return pltpu.make_async_copy(
            pieces.at[0, i, r], own.at[source, i, r], near_recv.at[i, r, source]
        )

    def halo_copy(i, r):
        return pltpu.make_async_remote_copy(
            src_ref=own.at[GROUP - 1, i, r],
            dst_ref=halo.at[i, r],
            send_sem=halo_send.at[i, r],
            recv_sem=halo_recv.at[i, r],
            device_id={"tm": (tm + GROUP) % 32},
            device_id_type=MESH,
        )

    def pass_on(i):
        for r in range(2):
            near_arrival(i, r, GROUP - 1).wait()

            @pl.when(block < 7)
            def _():
                halo_copy(i, r).start()

    def exchange(i, r):
        pltpu.make_async_copy(pieces.at[y, i, r], own.at[y, i, r], near_recv.at[i, r, y]).start()
        for offset in (1, 3, 2):
            near(i, r, offset).start()

    exchange(0, 0)
    loads[1].wait()
    split_inputs(1, voltages, spread, pieces)
    exchange(0, 1)

    @pl.when(y == GROUP - 1)
    def _():
        exchange(1, 0)
        exchange(1, 1)


    for offset in range(1, 8):
        pl.semaphore_signal(all_sem.at[0], inc=1, device_id=along_z(offset), device_id_type=MESH)
    pl.semaphore_wait(all_sem.at[0], 7)
    for offset in range(1, 4):
        pl.semaphore_signal(all_sem.at[1], inc=1, device_id=along_y(offset), device_id_type=MESH)

    for load in loads[2:]:
        load.wait()
    for i in range(2):
        delayed_tables(
            i, delays[2 * y + i], tap_all, turn_all, last_all, taps_ref, turn_ref, last_ref
        )
        if i == 0:
            pass_on(0)

    def far(l, i):
        return pltpu.make_async_remote_copy(
            src_ref=chunks.at[l, i],
            dst_ref=got.at[stn, me, i],
            send_sem=far_send,
            recv_sem=far_recv.at[block],
            device_id={"tm": l // 4, "ct": l % 4},
            device_id_type=MESH,
        )

    @pl.loop(0, 2)
    def _(i):
        for r in range(2):
            for source in range(GROUP - 1):
                near_arrival(i, r, source).wait()

            @pl.when((i == 0) & (y < GROUP - 1))
            def _():
                exchange(1, r)

        filter_frames(i, own, halo, taps_ref, xs, branch, False)
        slow_transform(i, turn_ref, branch, inner, False)

        @pl.when(i == 0)
        def _():
            pass_on(1)

        @pl.when(block > 0)
        def _():
            for r in range(2):
                halo_copy(i, r).wait_recv()

        filter_frames(i, own, halo, taps_ref, xs, branch, True)
        slow_transform(i, turn_ref, branch, inner, True)
        fast_transform(i, last_ref, inner, flat)

        @pl.when(i == 0)
        def _():
            pl.semaphore_wait(all_sem.at[1], 3)

        @pl.loop(0, OWNERS, step=4)
        def _(j0):
            for u in range(4):
                l = (me + j0 + u) % OWNERS
                rows = pl.ds(pl.multiple_of(l * 16, 16), 16)
                for r in range(2):
                    chunks[l, i, r, :, :] = flat[r, rows, :].astype(jnp.bfloat16)

            @pl.when(j0 == 0)
            def _():
                pltpu.make_async_copy(
                    chunks.at[me, i], got.at[stn, me, i], far_recv.at[block]
                ).start()

            @pl.when(j0 > 0)
            def _():
                far((me + j0) % OWNERS, i).start()

            for u in range(1, 4):
                far((me + j0 + u) % OWNERS, i).start()

    def twin(p):
        rows = got.at[stn, pl.ds(p * 16, 16)]
        return pltpu.make_async_remote_copy(
            src_ref=rows,
            dst_ref=rows,
            send_sem=twin_send.at[p],
            recv_sem=twin_recv.at[p],
            device_id={"stn": 1 - stn},
            device_id_type=MESH,
        )

    def turn(step):
        return (block + 7 - step) % 8

    def hand_over(step):
        rows = got.at[stn, pl.ds(turn(step) * 16, 16)]
        pltpu.make_async_copy(rows, rows, far_recv.at[turn(step)]).wait()
        twin(turn(step)).start()

    def take(step):
        twin(turn(step)).wait_recv()
        widen(turn(step), got, wide)

    hand_over(0)

    @pl.loop(0, 6)
    def _(step):
        @pl.when(step < 5)
        def _():
            hand_over(step + 1)

        take(step)
        reorder_all(step, wide, packed)

    first_six(stn, packed, sums)
    hand_over(6)
    hand_over(7)
    take(6)
    reorder_all(6, wide, packed)
    take(7)
    last_two(stn, wide, packed, sums, out_ref)

    for i in range(2):
        for r in range(2):
            for offset in (1, 3, 2):
                near(i, r, offset).wait_send()

            @pl.when(block < 7)
            def _():
                halo_copy(i, r).wait_send()

    for p in range(8):
        twin(p).wait_send()
    sent = chunks.at[pl.ds(0, OWNERS - 1)]
    pltpu.make_async_copy(sent, sent, far_send).wait()


def on_device(voltages, delays):
    dma = pltpu.SemaphoreType.DMA
    f32, bf16 = jnp.float32, jnp.bfloat16
    return pl.pallas_call(
        whole_kernel,
        out_shape=jax.ShapeDtypeStruct((2, SLOW, 32, 64), f32),
        in_specs=[pl.BlockSpec(memory_space=pltpu.SMEM)] + [pl.BlockSpec(memory_space=pl.ANY)] * 4,
        out_specs=pl.BlockSpec(memory_space=pltpu.VMEM),
        scratch_shapes=[
            pltpu.VMEM((2, 8, BLOCK * CHANNELS), bf16),
            pltpu.VMEM((SLOW, TAPS, FAST), f32),
            pltpu.VMEM((SLOW, 2 * SLOW, FAST), f32),
            pltpu.VMEM((2 * FAST, 2 * FAST), f32),
            pltpu.VMEM((2, SLOW, 24, FAST), f32),
            pltpu.VMEM((2, 2 * SLOW, FAST), f32),
            pltpu.VMEM((2, 2 * FAST, 2 * FAST), bf16),
            pltpu.VMEM((2, 8 * BLOCK + BLOCK, FAST), f32),
            pltpu.VMEM((GROUP, 2, 2, BLOCK, CHANNELS), bf16),
            pltpu.VMEM((GROUP, 2, 2, BLOCK, CHANNELS), bf16),
            pltpu.VMEM((2, 2, BLOCK, CHANNELS), bf16),
            pltpu.VMEM((OWNERS, 2, 2, 16, FAST), bf16),
            pltpu.VMEM((2, OWNERS, 2, 2, 16, FAST), bf16),
            pltpu.VMEM((2, 64, FAST), f32),
            pltpu.VMEM((2, SLOW, 64, FAST), f32),
            pltpu.VMEM((SLOW, 64, 2 * FAST), f32),
            pltpu.VMEM((2, FAST * 16 + 16, FAST), f32),
            pltpu.VMEM((2, 64 * 16 + 16, FAST), f32),
            pltpu.VMEM((16, FAST, 8 * FAST), bf16),
            pltpu.VMEM((16, FAST, FAST), f32),
            dma((5,)),
            pltpu.SemaphoreType.REGULAR((2,)),
            dma((2, 2, GROUP)),
            dma((2, 2, GROUP)),
            dma((2, 2)),
            dma((2, 2)),
            dma,
            dma((8,)),
            dma((8,)),
            dma((8,)),
        ],
        compiler_params=pltpu.CompilerParams(
            collective_id=0, has_side_effects=True, vmem_limit_bytes=56 << 20
        ),
    )(delays, voltages, tap_blocks(), turn_blocks(), last_table())


def solution(mesh):
    return jax.shard_map(
        on_device,
        mesh=mesh,
        in_specs=(P(None, ("stn", "ct"), "tm"), P(("stn", "ct"))),
        out_specs=P(None, ("tm", "ct"), "stn", None),
        check_vma=False,
    )
```
